256 devices in a mesh: band: 8 (over x_lo, y), sector: 32 (over x_hi, z, core).
Axes of the slice: x: 4 (x_hi: 2, x_lo: 2; x = x_hi * 2 + x_lo), y: 4, z: 8, core: 2. Of those that a mesh axis runs over, the one named last changes fastest.
Arguments:
- grid_lat: bfloat16 [64, 2048, 512], P('band', 'sector'), may hold values from -6 to 6
- mesh_lat: bfloat16 [32768, 512], P(('band', 'sector')), may hold values from -6 to 6
- edge_feat: bfloat16 [393216, 512], P(('band', 'sector')), may hold values from -24 to 24
- edge_src: int32 [393216], P(('band', 'sector')), may hold values from 0 to 255, as said below
- edge_dst: int32 [393216], P(('band', 'sector')), may hold values from 0 to 511, as said below
- send_rows: int32 [32768], P(('band', 'sector')), may hold values from 0 to 127
- w_edge1: bfloat16 [1536, 512], replicated, may hold values from -0.15625 to 0.15625
- w_edge2: bfloat16 [512, 512], replicated, may hold values from -0.25 to 0.25
- edge_gain: float32 [512], replicated, may hold values from 0.25 to 1.75
- w_node1: bfloat16 [1024, 512], replicated, may hold values from -0.1875 to 0.1875
- w_node2: bfloat16 [512, 512], replicated, may hold values from -0.25 to 0.25
- node_gain: float32 [512], replicated, may hold values from 0.25 to 1.75
- cotangent: bfloat16 [64, 2048, 512], P('band', 'sector'), may hold values from -6 to 6
Outputs:
- grid_out: bfloat16 [64, 2048, 512], P('band', 'sector')
- grad_grid: bfloat16 [64, 2048, 512], P('band', 'sector')
- grad_mesh: bfloat16 [32768, 512], P(('band', 'sector'))
- grad_w_edge1: float32 [1536, 512], P('sector')
The draws below stay inside these ranges and needn't reach their ends.
Inputs may be any that keep to these rules, and one draw needn't show every extreme that they name: `edge_src`: A device's mesh table is its 128 own rows followed by 32 rows each from the sector neighbour below, the sector neighbour above, the band neighbour below and the band neighbour above; devices of the first band never read the rows from below, those of the last band never the rows from above. `edge_dst`: each grid point of a device is the destination of exactly 3 of that device's edges; edges are in no particular order.
All inputs are finite; a program needn't handle non-finite values.
Results may differ from the reference program's by a relative error of at most 0.02.
Values may be sent and summed in bfloat16 or wider, within the bound.
No kernel may reach another device: no remote copies, remote signals or barrier semaphores. Data moves between devices by JAX's collectives and lax.ppermute only.
A program may use at most 64 MiB of HBM per device.

```python
import math
import jax
import jax.numpy as jnp
from jax import lax

D = 512
LAT_DEV = 8
LON_DEV = 64
MESH_DEV = 128
HALO = 32
GRID_DEV = 512
EDGE_DEV = 1536
TABLE = 256
BANDS = 8
SECTORS = 32
LAT = 64
LON = 2048
EDGES = 393216
MESH = 32768
SENDS = 32768
N_BAND = 8
N_SECTOR = 32
DEVICES = 256


def draw_edge_src(key, part):
    picked_rows = jax.random.randint(key, (DEVICES, EDGE_DEV), 0, MESH_DEV + 4 * HALO)
    band_index = (jnp.arange(DEVICES) // SECTORS)[:, None]
    below_start = MESH_DEV + 2 * HALO
    above_start = MESH_DEV + 3 * HALO
    first_band = (band_index == 0) & (picked_rows >= below_start) & (picked_rows < above_start)
    last_band = (band_index == BANDS - 1) & (picked_rows >= above_start)
    picked_rows = jnp.where(first_band, picked_rows - below_start, picked_rows)
    picked_rows = jnp.where(last_band, picked_rows - above_start, picked_rows)
    return picked_rows.reshape(-1).astype(jnp.int32)


def shuffled_order(subkey):
    return jax.random.permutation(subkey, EDGE_DEV)


def draw_edge_dst(key, part):
    subkeys = jax.random.split(key, DEVICES)
    orders = jax.vmap(shuffled_order)(subkeys)
    return (orders // 3).reshape(-1).astype(jnp.int32)


def place_ends(drawn, key, least, largest):
    spot = [jax.random.randint(jax.random.fold_in(key, axis), (), 0, length) for axis, length in enumerate(drawn.shape)]
    main_axis = drawn.shape.index(max(drawn.shape))
    neighbour = spot[:main_axis] + [(spot[main_axis] + 1) % drawn.shape[main_axis]] + spot[main_axis + 1:]
    return drawn.at[tuple(spot)].set(least).at[tuple(neighbour)].set(largest)


def strengthened(array, rng, source, target, parts, factor):
    owner, partner = [(jnp.arange(array.shape[position]) // (array.shape[position] // parts)).reshape([-1 if axis == position else 1 for axis in range(array.ndim)]) for position in (source, target)]
    chosen = jax.random.permutation(rng, parts)[partner]
    strong = (owner == chosen) | (owner == (partner + parts // 2) % parts)
    return jnp.where(strong, factor * array, array)


def steps_of(own_key, extent, cuts, least, largest):
    loudness, own = 1.0, jax.random.fold_in(own_key, 6)
    for axis_at, shards_of in cuts:
        draws = jnp.exp(jax.random.uniform(jax.random.fold_in(own, axis_at), (shards_of,), jnp.float32, least / len(cuts), largest / len(cuts)))
        loudness = loudness * jnp.repeat(draws, extent[axis_at] // shards_of).reshape([-1 if axis == axis_at else 1 for axis in range(len(extent))])
    return loudness


def normal_values(own_key, dims, deviation, bound, pieces=(), held_as=jnp.bfloat16):
    level = steps_of(own_key, dims, pieces, -0.22, 0.18) if pieces else 1.0
    array = jax.random.normal(own_key, dims, jnp.float32) * deviation * level
    return jnp.minimum(jnp.maximum(array, -bound), bound).astype(held_as)


def noise_with(key, shape, width, reach, cuts, heavy, kind=jnp.bfloat16):
    drawn = width * jax.random.normal(key, shape, jnp.float32)
    if cuts:
        drawn = drawn * steps_of(key, shape, cuts, -0.22, 0.18)
    return jnp.clip(strengthened(drawn, jax.random.fold_in(key, 3), *heavy), -reach, reach).astype(kind)


def setup_inputs(seed: int = 0) -> dict:
    key_of = jax.random.split(jax.random.key(seed), 14)
    return {
        "grid_lat": normal_values(key_of[0], (LAT, LON, D), 1.0, 6.0, ((0, 8), (1, 32))),
        "mesh_lat": normal_values(key_of[1], (MESH, D), 1.0, 6.0, ((0, 256),)),
        "edge_feat": noise_with(key_of[2], (EDGES, D), 1.0, 24.0, ((0, 256),), (0, 1, 256, 6.0)),
        "edge_src": draw_edge_src(jax.random.fold_in(key_of[13], 71), 0),
        "edge_dst": draw_edge_dst(jax.random.fold_in(key_of[13], 71), 0),
        "send_rows": place_ends(jax.random.randint(key_of[5], (SENDS,), 0, MESH_DEV), jax.random.fold_in(key_of[5], 1), 0, MESH_DEV - 1).astype(jnp.int32),
        "w_edge1": normal_values(key_of[6], (3 * D, D), (3 * D) ** -0.5, 0.15625),
        "w_edge2": normal_values(key_of[7], (D, D), D ** -0.5, 0.25),
        "edge_gain": jnp.clip(1.0 + 0.15 * jax.random.normal(key_of[8], (D,), jnp.float32), 0.25, 1.75),
        "w_node1": normal_values(key_of[9], (2 * D, D), (2 * D) ** -0.5, 0.1875),
        "w_node2": normal_values(key_of[10], (D, D), D ** -0.5, 0.25),
        "node_gain": jnp.clip(1.0 + 0.15 * jax.random.normal(key_of[11], (D,), jnp.float32), 0.25, 1.75),
        "cotangent": normal_values(key_of[12], (LAT, LON, D), 1.0, 6.0, ((0, 8), (1, 32))),
    }


EPSILON = 1e-05

def swish(values):
    return values * jax.nn.sigmoid(values)

def layer_norm(values, gain_vector):
    average = lax.optimization_barrier(jnp.mean(values, axis=-1, keepdims=True))
    centred = values - average
    spread = lax.optimization_barrier(jnp.mean(centred * centred, axis=-1, keepdims=True))
    return centred * lax.rsqrt(spread + EPSILON) * gain_vector

def decode_tail(pre_act, grid_wide, edge_dst, w_edge2, edge_gain, w_node1, w_node2, node_gain):
    hidden = swish(pre_act).astype(jnp.bfloat16)
    edge_raw = jnp.dot(hidden, w_edge2, preferred_element_type=jnp.float32)
    message = layer_norm(edge_raw, edge_gain).astype(jnp.bfloat16)
    points = grid_wide.shape[0]
    onehot = (edge_dst[None, :] == jnp.arange(points, dtype=jnp.int32)[:, None]).astype(jnp.bfloat16)
    aggregated = jnp.dot(onehot, message, preferred_element_type=jnp.float32).astype(jnp.bfloat16)
    node_input = jnp.concatenate([aggregated, grid_wide.astype(jnp.bfloat16)], axis=1)
    node_hidden = swish(jnp.dot(node_input, w_node1, preferred_element_type=jnp.float32)).astype(jnp.bfloat16)
    node_raw = jnp.dot(node_hidden, w_node2, preferred_element_type=jnp.float32)
    return (grid_wide + layer_norm(node_raw, node_gain)).astype(jnp.bfloat16)

def block_pass(mesh_table, grid_block, edge_block, edge_src, edge_dst, cot_block, w_edge1, w_edge2, edge_gain, w_node1, w_node2, node_gain):
    feature_width = w_edge2.shape[0]
    inputs = jnp.concatenate([edge_block, mesh_table[edge_src], grid_block[edge_dst]], axis=1)
    pre_act = jnp.dot(inputs, w_edge1, preferred_element_type=jnp.float32)
    grid_wide = grid_block.astype(jnp.float32)

    def finish(pre_values, grid_values):
        return decode_tail(pre_values, grid_values, edge_dst, w_edge2, edge_gain, w_node1, w_node2, node_gain)
    result, pullback = jax.vjp(finish, pre_act, grid_wide)
    grad_pre, grad_tail = pullback(cot_block)
    grad_pre_b = grad_pre.astype(jnp.bfloat16)
    grad_weight = lax.dot_general(inputs, grad_pre_b, (((0,), (0,)), ((), ())), preferred_element_type=jnp.float32)
    grad_inputs = lax.dot_general(grad_pre_b, w_edge1[feature_width:], (((1,), (1,)), ((), ())), preferred_element_type=jnp.float32)
    grad_table = jax.ops.segment_sum(grad_inputs[:, :feature_width], edge_src, num_segments=mesh_table.shape[0])
    grad_grid = grad_tail + jax.ops.segment_sum(grad_inputs[:, feature_width:], edge_dst, num_segments=grid_block.shape[0])
    return (result, grad_table, grad_grid, grad_weight)

def reference(grid_lat, mesh_lat, edge_feat, edge_src, edge_dst, send_rows, w_edge1, w_edge2, edge_gain, w_node1, w_node2, node_gain, cotangent):
    band_count = N_BAND
    sector_count = N_SECTOR
    blocks = band_count * sector_count
    feature_width = D
    mesh_blocks = mesh_lat.reshape(band_count, sector_count, MESH_DEV, feature_width)
    send_table = send_rows.reshape(band_count, sector_count, 4, HALO)

    def take_rows(rows_block, index_block):
        return rows_block[index_block]

    def select_part(part_index):
        return jax.vmap(jax.vmap(take_rows))(mesh_blocks, send_table[:, :, part_index, :])
    to_left = select_part(0)
    to_right = select_part(1)
    to_below = select_part(2)
    to_above = select_part(3)
    from_left = jnp.roll(to_right, 1, axis=1)
    from_right = jnp.roll(to_left, -1, axis=1)
    zero_rows = jnp.zeros_like(to_above[:1])
    from_below = jnp.concatenate([zero_rows, to_above[:-1]], axis=0)
    from_above = jnp.concatenate([to_below[1:], zero_rows], axis=0)
    tables = jnp.concatenate([mesh_blocks, from_left, from_right, from_below, from_above], axis=2)
    tables = tables.reshape(blocks, TABLE, feature_width)

    def to_blocks(field):
        shaped = field.reshape(band_count, LAT_DEV, sector_count, LON_DEV, feature_width)
        return shaped.transpose(0, 2, 1, 3, 4).reshape(blocks, GRID_DEV, feature_width)

    def from_blocks(field):
        shaped = field.reshape(band_count, sector_count, LAT_DEV, LON_DEV, feature_width)
        return shaped.transpose(0, 2, 1, 3, 4).reshape(LAT, LON, feature_width)
    grid_blocks = to_blocks(grid_lat)
    cot_blocks = to_blocks(cotangent)
    edge_blocks = edge_feat.reshape(blocks, EDGE_DEV, feature_width)
    src_blocks = edge_src.reshape(blocks, EDGE_DEV)
    dst_blocks = edge_dst.reshape(blocks, EDGE_DEV)

    def visit_block(running, block_items):
        mesh_table, grid_block, edge_block, src_block, dst_block, cot_block = block_items
        result, grad_table, grad_grid, grad_weight = block_pass(mesh_table, grid_block, edge_block, src_block, dst_block, cot_block, w_edge1, w_edge2, edge_gain, w_node1, w_node2, node_gain)
        return (running + grad_weight, (result, grad_table, grad_grid))
    start_sum = jnp.zeros((3 * feature_width, feature_width), jnp.float32)
    grad_weight, outputs = lax.scan(visit_block, start_sum, (tables, grid_blocks, edge_blocks, src_blocks, dst_blocks, cot_blocks))
    results, grad_tables, grad_grids = outputs
    grad_tables = grad_tables.reshape(band_count, sector_count, TABLE, feature_width)
    own_part = grad_tables[:, :, :MESH_DEV]
    grad_left = grad_tables[:, :, MESH_DEV:MESH_DEV + HALO]
    grad_right = grad_tables[:, :, MESH_DEV + HALO:MESH_DEV + 2 * HALO]
    grad_below = grad_tables[:, :, MESH_DEV + 2 * HALO:MESH_DEV + 3 * HALO]
    grad_above = grad_tables[:, :, MESH_DEV + 3 * HALO:]
    zero_grads = jnp.zeros_like(grad_above[:1])
    left_back = jnp.roll(grad_right, 1, axis=1)
    right_back = jnp.roll(grad_left, -1, axis=1)
    below_back = jnp.concatenate([zero_grads, grad_above[:-1]], axis=0)
    above_back = jnp.concatenate([grad_below[1:], zero_grads], axis=0)
    returned = jnp.concatenate([left_back, right_back, below_back, above_back], axis=2)
    send_index = send_rows.reshape(band_count, sector_count, 4 * HALO)

    def add_rows(values, index_block):
        return jax.ops.segment_sum(values, index_block, num_segments=MESH_DEV)
    scattered = jax.vmap(jax.vmap(add_rows))(returned, send_index)
    grad_mesh = (own_part + scattered).reshape(MESH, feature_width).astype(jnp.bfloat16)
    grid_out = from_blocks(results)
    grad_grid = from_blocks(grad_grids).astype(jnp.bfloat16)
    grad_w_edge1 = grad_weight * (1.0 / math.sqrt(EDGES))
    return (grid_out, grad_grid, grad_mesh, grad_w_edge1)
```

```python
import math

import jax
import jax.numpy as jnp
from jax import lax
from jax.experimental import pallas as pl
from jax.experimental.pallas import tpu as pltpu
from jax.sharding import PartitionSpec as P

EPSILON = 1e-05
BF16 = jnp.bfloat16
F32 = jnp.float32
ANY = pl.BlockSpec(memory_space=pl.ANY)
VM = pl.BlockSpec(memory_space=pltpu.VMEM)


def mm(a, b):
    return lax.dot_general(a, b, (((1,), (0,)), ((), ())), preferred_element_type=F32)


def mm_nt(a, b):
    return lax.dot_general(a, b, (((1,), (1,)), ((), ())), preferred_element_type=F32)


def mm_tn(a, b):
    return lax.dot_general(a, b, (((0,), (0,)), ((), ())), preferred_element_type=F32)


def onehot_rows(index_row, rows):
    n = index_row.shape[1]
    return (lax.broadcasted_iota(jnp.int32, (rows, n), 0) == index_row).astype(BF16)


def onehot_cols(index_col, cols):
    n = index_col.shape[0]
    return (lax.broadcasted_iota(jnp.int32, (n, cols), 1) == index_col).astype(BF16)


def column_of(index_row):
    n = index_row.shape[1]
    return jnp.transpose(jnp.broadcast_to(index_row, (8, n)))[:, 0:1]


def swish_parts(pre):
    sig = 0.5 * jnp.tanh(0.5 * pre) + 0.5
    value = pre * sig
    return value, sig + value * (1.0 - sig)


def norm_parts(raw):
    width = raw.shape[1]
    centred = raw - jnp.sum(raw, axis=1, keepdims=True) * (1.0 / width)
    spread = jnp.sum(centred * centred, axis=1, keepdims=True) * (1.0 / width)
    scale = lax.rsqrt(spread + EPSILON)
    return centred * scale, scale


def norm_back(grad, unit, scale):
    width = grad.shape[1]
    first = jnp.sum(grad, axis=1, keepdims=True) * (1.0 / width)
    second = jnp.sum(grad * unit, axis=1, keepdims=True) * (1.0 / width)
    return (grad - first - unit * second) * scale


def pick_kernel(send_ref, mesh_ref, *outs):
    rows = mesh_ref.shape[0]
    hot = onehot_rows(send_ref[...], rows)
    picked = mm_tn(hot, mesh_ref[...]).astype(BF16)
    margin = picked.shape[0] // 4
    for i, out in enumerate(outs):
        out[...] = picked[i * margin : (i + 1) * margin]


def pick(send_rows, mesh_lat):
    n, width = send_rows.shape[0], mesh_lat.shape[1]
    part = jax.ShapeDtypeStruct((n // 4, width), BF16)
    return pl.pallas_call(
        pick_kernel,
        out_shape=[part] * 4,
        in_specs=[VM, VM],
        out_specs=[VM] * 4,
        name="pick",
        cost_estimate=pl.CostEstimate(flops=2 * n * n * width, bytes_accessed=2 * n * width * 2, transcendentals=0),
    )(send_rows.reshape(1, n), mesh_lat)


TILE = 512


def early_kernel(dst_ref, grid_ref, edge_ref, w_edge_ref, w_grid_ref, w_node_ref, base_ref, node_ref, prod_ref):
    grid = grid_ref[...]
    width = grid.shape[1]
    prod_ref[...] = mm(grid, w_grid_ref[...]).astype(BF16)
    node_ref[...] = mm(grid, w_node_ref[...])
    points = grid.shape[0]
    for t in range(edge_ref.shape[0] // TILE):
        rows = slice(t * TILE, (t + 1) * TILE)
        hot = onehot_cols(column_of(dst_ref[:, rows]), points)
        base_ref[rows, :] = mm(edge_ref[rows, :], w_edge_ref[...]) + mm(hot, prod_ref[...])


def early(edge_dst, grid_block, edge_feat, w_edge1, w_node1):
    edges, width = edge_feat.shape
    points = grid_block.shape[0]
    block = lambda i: pl.BlockSpec((width, width), lambda k: (i, 0))
    return pl.pallas_call(
        early_kernel,
        out_shape=[
            jax.ShapeDtypeStruct((edges, width), F32),
            jax.ShapeDtypeStruct((points, width), F32),
        ],
        in_specs=[VM, VM, VM, block(0), block(2), block(1)],
        out_specs=[VM, VM],
        scratch_shapes=[pltpu.VMEM((points, width), BF16)],
        compiler_params=pltpu.CompilerParams(vmem_limit_bytes=40 << 20),
        grid=(1,),
        name="early",
        cost_estimate=pl.CostEstimate(
            flops=4 * edges * width * width + 4 * points * width * width,
            bytes_accessed=10 * edges * width,
            transcendentals=0,
        ),
    )(edge_dst.reshape(1, edges), grid_block, edge_feat, w_edge1, w_edge1, w_node1)


def main_kernel(
    src_ref,
    dst_ref,
    mesh_ref,
    r0_ref,
    r1_ref,
    r2_ref,
    r3_ref,
    eg_ref,
    ng_ref,
    base_hbm,
    node_hbm,
    edge_hbm,
    grid_hbm,
    cot_hbm,
    w1_hbm,
    w2_hbm,
    n1_hbm,
    n2_hbm,
    out_ref,
    dnpre_ref,
    sm_ref,
    sg_ref,
    gw_ref,
    base,
    node,
    edge,
    grid,
    cot,
    wm,
    w2,
    n1,
    n2,
    table,
    prod,
    hot_s,
    hot_d,
    hot_st,
    hot_dt,
    slope,
    unit,
    scale,
    msg,
    gp,
    sems,
):
    width = w2.shape[0]
    edges, points, rows_table = base.shape[0], grid.shape[0], table.shape[0]
    tiles = [slice(t * TILE, (t + 1) * TILE) for t in range(edges // TILE)]
    copies = [
        pltpu.make_async_copy(w1_hbm.at[pl.ds(width, width), :], wm, sems.at[0]),
        pltpu.make_async_copy(base_hbm, base, sems.at[1]),
        pltpu.make_async_copy(w2_hbm, w2, sems.at[2]),
        pltpu.make_async_copy(n1_hbm.at[pl.ds(0, width), :], n1, sems.at[3]),
        pltpu.make_async_copy(node_hbm, node, sems.at[4]),
        pltpu.make_async_copy(n2_hbm, n2, sems.at[5]),
        pltpu.make_async_copy(cot_hbm, cot, sems.at[6]),
        pltpu.make_async_copy(grid_hbm, grid, sems.at[7]),
        pltpu.make_async_copy(edge_hbm, edge, sems.at[8]),
    ]
    for copy in copies:
        copy.start()
    own, margin = mesh_ref.shape[0], r0_ref.shape[0]
    table[0:own, :] = mesh_ref[...]
    for i, part in enumerate((r0_ref, r1_ref, r2_ref, r3_ref)):
        table[own + i * margin : own + (i + 1) * margin, :] = part[...]
    hot_s[...] = onehot_cols(column_of(src_ref[...]), rows_table)
    hot_d[...] = onehot_cols(column_of(dst_ref[...]), points)
    hot_st[...] = onehot_rows(src_ref[...], rows_table)
    hot_dt[...] = onehot_rows(dst_ref[...], points)
    edge_gain, node_gain = eg_ref[...], ng_ref[...]

    copies[0].wait()
    prod[...] = mm(table[...], wm[...]).astype(BF16)
    copies[1].wait()
    copies[2].wait()
    for rows in tiles:
        pre = base[rows, :] + mm(hot_s[rows, :], prod[...])
        hidden, steep = swish_parts(pre)
        slope[rows, :] = steep
        normed, inv = norm_parts(mm(hidden.astype(BF16), w2[...]))
        unit[rows, :] = normed
        scale[rows, :] = inv
        msg[rows, :] = (normed * edge_gain).astype(BF16)
    for copy in copies[3:8]:
        copy.wait()
    agg = mm(hot_dt[...], msg[...]).astype(BF16)
    node_hidden, node_slope = swish_parts(mm(agg, n1[...]) + node[...])
    node_unit, node_inv = norm_parts(mm(node_hidden.astype(BF16), n2[...]))
    out_ref[...] = (grid[...].astype(F32) + node_unit * node_gain).astype(BF16)
    d_raw = norm_back(cot[...].astype(F32) * node_gain, node_unit, node_inv)
    d_hidden = mm_nt(d_raw.astype(BF16), n2[...]).astype(BF16).astype(F32)
    d_pre = (d_hidden * node_slope).astype(BF16)
    dnpre_ref[...] = d_pre
    d_agg = mm_nt(d_pre, n1[...]).astype(BF16)
    for rows in tiles:
        d_msg = mm(hot_d[rows, :], d_agg)
        d_edge = norm_back(d_msg * edge_gain, unit[rows, :], scale[rows, :])
        d_hid = mm_nt(d_edge.astype(BF16), w2[...]).astype(BF16).astype(F32)
        gp[rows, :] = (d_hid * slope[rows, :]).astype(BF16)
    copies[8].wait()
    gw_ref[0:width, :] = mm_tn(edge[...], gp[...]).astype(BF16)
    sm = mm(hot_st[...], gp[...]).astype(BF16)
    sm_ref[...] = sm
    gw_ref[width : 2 * width, :] = mm_tn(table[...], sm).astype(BF16)
    sg = mm(hot_dt[...], gp[...]).astype(BF16)
    sg_ref[...] = sg
    gw_ref[2 * width : 3 * width, :] = mm_tn(grid[...], sg).astype(BF16)


def main(edge_src, edge_dst, mesh_lat, received, edge_gain, node_gain, base, node, edge_feat, grid_block, cot_block, w1, w2, n1, n2):
    edges, width = edge_feat.shape
    points = grid_block.shape[0]
    table = mesh_lat.shape[0] + 4 * received[0].shape[0]
    sds = jax.ShapeDtypeStruct
    square = pltpu.VMEM((width, width), BF16)
    nodes = pltpu.VMEM((points, width), BF16)
    return pl.pallas_call(
        main_kernel,
        out_shape=[
            sds((points, width), BF16),
            sds((points, width), BF16),
            sds((table, width), BF16),
            sds((points, width), BF16),
            sds((3 * width, width), BF16),
        ],
        in_specs=[VM] * 9 + [ANY] * 9,
        out_specs=[VM] * 5,
        scratch_shapes=[
            pltpu.VMEM((edges, width), F32),
            pltpu.VMEM((points, width), F32),
            pltpu.VMEM((edges, width), BF16),
            nodes,
            nodes,
            square,
            square,
            square,
            square,
            pltpu.VMEM((table, width), BF16),
            pltpu.VMEM((table, width), BF16),
            pltpu.VMEM((edges, table), BF16),
            pltpu.VMEM((edges, points), BF16),
            pltpu.VMEM((table, edges), BF16),
            pltpu.VMEM((points, edges), BF16),
            pltpu.VMEM((edges, width), F32),
            pltpu.VMEM((edges, width), F32),
            pltpu.VMEM((edges, 1), F32),
            pltpu.VMEM((edges, width), BF16),
            pltpu.VMEM((edges, width), BF16),
            pltpu.SemaphoreType.DMA((9,)),
        ],
        compiler_params=pltpu.CompilerParams(vmem_limit_bytes=56 << 20),
        name="main",
        cost_estimate=pl.CostEstimate(
            flops=16 * edges * width * width,
            bytes_accessed=14 * edges * width,
            transcendentals=edges * width,
        ),
    )(
        edge_src.reshape(1, edges),
        edge_dst.reshape(1, edges),
        mesh_lat,
        *received,
        edge_gain.reshape(1, width),
        node_gain.reshape(1, width),
        base,
        node,
        edge_feat,
        grid_block,
        cot_block,
        w1,
        w2,
        n1,
        n2,
    )


def table_kernel(sm_ref, w_ref, own_ref, *outs):
    grad = mm_nt(sm_ref[...], w_ref[...])
    own, margin = own_ref.shape[0], outs[0].shape[0]
    own_ref[...] = grad[0:own]
    for i, out in enumerate(outs):
        out[...] = grad[own + i * margin : own + (i + 1) * margin].astype(BF16)


def table_grads(sm, w1, own, margin):
    width = sm.shape[1]
    sds = jax.ShapeDtypeStruct
    return pl.pallas_call(
        table_kernel,
        out_shape=[sds((own, width), F32)] + [sds((margin, width), BF16)] * 4,
        in_specs=[VM, pl.BlockSpec((width, width), lambda k: (1, 0))],
        out_specs=[VM] * 5,
        grid=(1,),
        name="table_grads",
        cost_estimate=pl.CostEstimate(flops=2 * sm.shape[0] * width * width, bytes_accessed=1 << 20, transcendentals=0),
    )(sm, w1)


def grid_kernel(sg_ref, w1_ref, dnpre_ref, n1_ref, cot_ref, out_ref):
    total = cot_ref[...].astype(F32) + mm_nt(dnpre_ref[...], n1_ref[...]) + mm_nt(sg_ref[...], w1_ref[...])
    out_ref[...] = total.astype(BF16)


def grid_grads(sg, w1, dnpre, n1, cot_block):
    points, width = sg.shape
    return pl.pallas_call(
        grid_kernel,
        out_shape=jax.ShapeDtypeStruct((points, width), BF16),
        in_specs=[VM, pl.BlockSpec((width, width), lambda k: (2, 0)), VM, pl.BlockSpec((width, width), lambda k: (1, 0)), VM],
        out_specs=VM,
        grid=(1,),
        name="grid_grads",
        cost_estimate=pl.CostEstimate(flops=4 * points * width * width, bytes_accessed=3 << 20, transcendentals=0),
    )(sg, w1, dnpre, n1, cot_block)


def mesh_kernel(send_ref, own_ref, r0_ref, r1_ref, r2_ref, r3_ref, out_ref):
    own = own_ref.shape[0]
    hot = onehot_rows(send_ref[...], own)
    margin = r0_ref.shape[0]
    total = own_ref[...]
    for i, part in enumerate((r0_ref, r1_ref, r2_ref, r3_ref)):
        total = total + mm(hot[:, i * margin : (i + 1) * margin], part[...])
    out_ref[...] = total.astype(BF16)


def mesh_grads(send_rows, own, returned):
    n = send_rows.shape[0]
    return pl.pallas_call(
        mesh_kernel,
        out_shape=jax.ShapeDtypeStruct(own.shape, BF16),
        in_specs=[VM] * 6,
        out_specs=VM,
        name="mesh_grads",
        cost_estimate=pl.CostEstimate(flops=2 * n * n * own.shape[1], bytes_accessed=1 << 19, transcendentals=0),
    )(send_rows.reshape(1, n), own, *returned)


def steps(axis, wrap):
    devices = lax.axis_size(axis)
    up = [(i, (i + 1) % devices) for i in range(devices if wrap else devices - 1)]
    return up, [(j, i) for i, j in up]


def swap(parts):
    sector_up, sector_down = steps("sector", True)
    band_up, band_down = steps("band", False)
    return [
        lax.ppermute(parts[1], "sector", sector_up),
        lax.ppermute(parts[0], "sector", sector_down),
        lax.ppermute(parts[3], "band", band_up),
        lax.ppermute(parts[2], "band", band_down),
    ]


def reduce_weights(gw):
    sectors = lax.axis_size("sector")
    parts = lax.all_to_all(gw.reshape(sectors, gw.shape[0] // sectors, gw.shape[1]), "sector", 0, 0)
    part = jnp.sum(parts.astype(F32), axis=0).astype(BF16)
    bands = lax.axis_size("band")
    others = [lax.ppermute(part, "band", [(i, i ^ d) for i in range(bands)]) for d in range(1, bands)]
    total = part.astype(F32)
    for other in others:
        total = total + other.astype(F32)
    return total


def shards(
    grid_lat,
    mesh_lat,
    edge_feat,
    edge_src,
    edge_dst,
    send_rows,
    w_edge1,
    w_edge2,
    edge_gain,
    w_node1,
    w_node2,
    node_gain,
    cotangent,
):
    lat_rows, lon_cols, width = grid_lat.shape
    grid_block = grid_lat.reshape(lat_rows * lon_cols, width)
    cot_block = cotangent.reshape(lat_rows * lon_cols, width)
    own, margin = mesh_lat.shape[0], send_rows.shape[0] // 4
    received = swap(pick(send_rows, mesh_lat))
    base, node = early(edge_dst, grid_block, edge_feat, w_edge1, w_node1)
    result, dnpre, sm, sg, gw = main(
        edge_src, edge_dst, mesh_lat, received, edge_gain, node_gain, base, node, edge_feat, grid_block, cot_block, w_edge1, w_edge2, w_node1, w_node2
    )
    own_grad, *borrowed = table_grads(sm, w_edge1, own, margin)
    returned = swap(borrowed)
    grad_grid = grid_grads(sg, w_edge1, dnpre, w_node1, cot_block)
    grad_mesh = mesh_grads(send_rows, own_grad, returned)
    total_edges = edge_feat.shape[0] * lax.axis_size("band") * lax.axis_size("sector")
    grad_w = reduce_weights(gw) * (1.0 / math.sqrt(total_edges))
    return (
        result.reshape(lat_rows, lon_cols, width),
        grad_grid.reshape(lat_rows, lon_cols, width),
        grad_mesh,
        grad_w,
    )


def solution(mesh):
    rows = P(("band", "sector"), None)
    flat = P(("band", "sector"))
    grid = P("band", "sector", None)
    in_specs = (grid, rows, rows, flat, flat, flat, P(), P(), P(), P(), P(), P(), grid)
    out_specs = (grid, grid, rows, P("sector", None))
    return jax.shard_map(shards, mesh=mesh, in_specs=in_specs, out_specs=out_specs, check_vma=False)
```

```python
import math

import jax
import jax.numpy as jnp
from jax import lax
from jax.experimental import pallas as pl
from jax.experimental.pallas import tpu as pltpu
from jax.sharding import PartitionSpec as P

EPSILON = 1e-05
BF16 = jnp.bfloat16
F32 = jnp.float32
ANY = pl.BlockSpec(memory_space=pl.ANY)
VM = pl.BlockSpec(memory_space=pltpu.VMEM)


def mm(a, b):
    return lax.dot_general(a, b, (((1,), (0,)), ((), ())), preferred_element_type=F32)


def mm_nt(a, b):
    return lax.dot_general(a, b, (((1,), (1,)), ((), ())), preferred_element_type=F32)


def mm_tn(a, b):
    return lax.dot_general(a, b, (((0,), (0,)), ((), ())), preferred_element_type=F32)


def onehot_rows(index_row, rows):
    n = index_row.shape[1]
    return (lax.broadcasted_iota(jnp.int32, (rows, n), 0) == index_row).astype(BF16)


def onehot_cols(index_col, cols):
    n = index_col.shape[0]
    return (lax.broadcasted_iota(jnp.int32, (n, cols), 1) == index_col).astype(BF16)


LANES = 128


def fill_rows(index_ref, hot_ref):
    for j in range(index_ref.shape[0]):
        hot_ref[:, j * LANES : (j + 1) * LANES] = onehot_rows(index_ref[j : j + 1, :], hot_ref.shape[0])


def fill_cols(index_ref, hot_ref):
    turned = jnp.transpose(index_ref[...])
    for j in range(index_ref.shape[0]):
        hot_ref[j * LANES : (j + 1) * LANES, :] = onehot_cols(turned[:, j : j + 1], hot_ref.shape[1])


def swish_parts(pre):
    sig = 0.5 * jnp.tanh(0.5 * pre) + 0.5
    value = pre * sig
    return value, sig + value * (1.0 - sig)


def norm_parts(raw):
    width = raw.shape[1]
    centred = raw - jnp.sum(raw, axis=1, keepdims=True) * (1.0 / width)
    spread = jnp.sum(centred * centred, axis=1, keepdims=True) * (1.0 / width)
    scale = lax.rsqrt(spread + EPSILON)
    return centred * scale, scale


def norm_back(grad, unit, scale):
    width = grad.shape[1]
    first = jnp.sum(grad, axis=1, keepdims=True) * (1.0 / width)
    second = jnp.sum(grad * unit, axis=1, keepdims=True) * (1.0 / width)
    return (grad - first - unit * second) * scale


def parity(axis):
    return lax.axis_index(axis) % 2


def pick_kernel(send_ref, mesh_ref, *refs):
    outs, picked = refs[:4], refs[4]
    hot = onehot_rows(send_ref[...], mesh_ref.shape[0])
    picked[...] = mm_tn(hot, mesh_ref[...]).astype(BF16)
    margin = outs[0].shape[0]
    for pair, axis in enumerate(("sector", "band")):
        odd = parity(axis)
        for turn in range(2):
            group = 2 * pair + (1 - odd if turn == 0 else odd)
            outs[2 * pair + turn][...] = picked[pl.ds(pl.multiple_of(group * margin, margin), margin), :]


def pick(send_rows, mesh_lat):
    n, width = send_rows.shape[0], mesh_lat.shape[1]
    part = jax.ShapeDtypeStruct((n // 4, width), BF16)
    return pl.pallas_call(
        pick_kernel,
        out_shape=[part] * 4,
        in_specs=[VM, VM],
        out_specs=[VM] * 4,
        scratch_shapes=[pltpu.VMEM((n, width), BF16)],
        name="pick",
        cost_estimate=pl.CostEstimate(flops=2 * n * n * width, bytes_accessed=2 * n * width * 2, transcendentals=0),
    )(send_rows.reshape(1, n), mesh_lat)


TILE = 512


def early_kernel(
    dst_ref, grid_hbm, edge_hbm, w1_hbm, n1_hbm, base_hbm, node_hbm, grid, edge, w_edge, w_grid, w_node, prod, hot, base, node, sems
):
    width = grid.shape[1]
    edges = edge.shape[0]
    tiles = [pl.ds(t * TILE, TILE) for t in range(edges // TILE)]
    copies = [
        pltpu.make_async_copy(grid_hbm, grid, sems.at[0]),
        pltpu.make_async_copy(w1_hbm.at[pl.ds(2 * width, width), :], w_grid, sems.at[1]),
        pltpu.make_async_copy(n1_hbm.at[pl.ds(width, width), :], w_node, sems.at[2]),
        pltpu.make_async_copy(w1_hbm.at[pl.ds(0, width), :], w_edge, sems.at[3]),
    ]
    loads = [pltpu.make_async_copy(edge_hbm.at[rows, :], edge.at[rows, :], sems.at[4 + t]) for t, rows in enumerate(tiles)]
    for copy in copies + loads:
        copy.start()
    fill_cols(dst_ref, hot)
    copies[0].wait()
    copies[1].wait()
    prod[...] = mm(grid[...], w_grid[...]).astype(BF16)
    copies[2].wait()
    node[...] = mm(grid[...], w_node[...])
    stores = [pltpu.make_async_copy(node, node_hbm, sems.at[4 + len(tiles)])]
    stores[0].start()
    copies[3].wait()
    for t, rows in enumerate(tiles):
        loads[t].wait()
        base[rows, :] = mm(edge[rows, :], w_edge[...]) + mm(hot[rows, :], prod[...])
        store = pltpu.make_async_copy(base.at[rows, :], base_hbm.at[rows, :], sems.at[5 + len(tiles) + t])
        store.start()
        stores.append(store)
    for store in stores:
        store.wait()


def early(edge_dst, grid_block, edge_feat, w_edge1, w_node1):
    edges, width = edge_feat.shape
    points = grid_block.shape[0]
    square = pltpu.VMEM((width, width), BF16)
    return pl.pallas_call(
        early_kernel,
        out_shape=[
            jax.ShapeDtypeStruct((edges, width), F32),
            jax.ShapeDtypeStruct((points, width), F32),
        ],
        in_specs=[VM] + [ANY] * 4,
        out_specs=[ANY, ANY],
        scratch_shapes=[
            pltpu.VMEM((points, width), BF16),
            pltpu.VMEM((edges, width), BF16),
            square,
            square,
            square,
            pltpu.VMEM((points, width), BF16),
            pltpu.VMEM((edges, points), BF16),
            pltpu.VMEM((edges, width), F32),
            pltpu.VMEM((points, width), F32),
            pltpu.SemaphoreType.DMA((5 + 2 * (edges // TILE),)),
        ],
        compiler_params=pltpu.CompilerParams(vmem_limit_bytes=58 << 20),
        name="early",
        cost_estimate=pl.CostEstimate(
            flops=4 * edges * width * width + 4 * points * width * width,
            bytes_accessed=10 * edges * width,
            transcendentals=0,
        ),
    )(edge_dst.reshape(edges // LANES, LANES), grid_block, edge_feat, w_edge1, w_node1)


def gray(value):
    return value ^ (value >> 1)


def piece_order():
    pieces = []
    for block in range(16):
        code = (block >> 3) | ((block >> 2) & 1) << 1 | ((block >> 1) & 1) << 2
        z = next(i for i in range(8) if gray(i) == code)
        pieces.append((block & 1) * 8 + z)
    return pieces


def main_kernel(
    src_ref,
    dst_ref,
    mesh_ref,
    r0_ref,
    r1_ref,
    r2_ref,
    r3_ref,
    eg_ref,
    ng_ref,
    base_hbm,
    node_hbm,
    edge_hbm,
    grid_hbm,
    cot_hbm,
    w1_hbm,
    w2_hbm,
    n1_hbm,
    n2_hbm,
    out_ref,
    dnpre_ref,
    sg_ref,
    own_ref,
    b0_ref,
    b1_ref,
    b2_ref,
    b3_ref,
    send_a,
    send_b,
    keep_a,
    keep_b,
    base,
    node,
    edge,
    grid,
    cot,
    wm,
    w2,
    n1,
    n2,
    table,
    prod,
    hot_s,
    hot_d,
    hot_st,
    hot_dt,
    slope,
    unit,
    scale,
    msg,
    gp,
    gw,
    borrowed,
    sems,
):
    width = w2.shape[0]
    edges, points, rows_table = base.shape[0], grid.shape[0], table.shape[0]
    tiles = [slice(t * TILE, (t + 1) * TILE) for t in range(edges // TILE)]
    copies = [
        pltpu.make_async_copy(w1_hbm.at[pl.ds(width, width), :], wm, sems.at[0]),
        pltpu.make_async_copy(base_hbm, base, sems.at[1]),
        pltpu.make_async_copy(w2_hbm, w2, sems.at[2]),
        pltpu.make_async_copy(n1_hbm.at[pl.ds(0, width), :], n1, sems.at[3]),
        pltpu.make_async_copy(node_hbm, node, sems.at[4]),
        pltpu.make_async_copy(n2_hbm, n2, sems.at[5]),
        pltpu.make_async_copy(cot_hbm, cot, sems.at[6]),
        pltpu.make_async_copy(grid_hbm, grid, sems.at[7]),
        pltpu.make_async_copy(edge_hbm, edge, sems.at[8]),
    ]
    for copy in copies:
        copy.start()
    own, margin = mesh_ref.shape[0], r0_ref.shape[0]
    table[0:own, :] = mesh_ref[...]
    starts = []
    for pair, axis in enumerate(("sector", "band")):
        odd = parity(axis)
        for slot in (1 - odd, odd):
            starts.append(pl.multiple_of((2 * pair + slot) * margin, margin))
    for start, part in zip(starts, (r0_ref, r1_ref, r2_ref, r3_ref)):
        table[pl.ds(own + start, margin), :] = part[...]
    fill_cols(src_ref, hot_s)
    fill_cols(dst_ref, hot_d)
    fill_rows(src_ref, hot_st)
    fill_rows(dst_ref, hot_dt)
    edge_gain, node_gain = eg_ref[...], ng_ref[...]

    copies[0].wait()
    prod[...] = mm(table[...], wm[...]).astype(BF16)
    copies[1].wait()
    copies[2].wait()
    for rows in tiles:
        pre = base[rows, :] + mm(hot_s[rows, :], prod[...])
        hidden, steep = swish_parts(pre)
        slope[rows, :] = steep
        normed, inv = norm_parts(mm(hidden.astype(BF16), w2[...]))
        unit[rows, :] = normed
        scale[rows, :] = inv
        msg[rows, :] = (normed * edge_gain).astype(BF16)
    for copy in copies[3:8]:
        copy.wait()
    agg = mm(hot_dt[...], msg[...]).astype(BF16)
    node_hidden, node_slope = swish_parts(mm(agg, n1[...]) + node[...])
    node_unit, node_inv = norm_parts(mm(node_hidden.astype(BF16), n2[...]))
    out_ref[...] = (grid[...].astype(F32) + node_unit * node_gain).astype(BF16)
    d_raw = norm_back(cot[...].astype(F32) * node_gain, node_unit, node_inv)
    d_hidden = mm_nt(d_raw.astype(BF16), n2[...]).astype(BF16).astype(F32)
    d_pre = (d_hidden * node_slope).astype(BF16)
    dnpre_ref[...] = d_pre
    d_agg = mm_nt(d_pre, n1[...]).astype(BF16)
    for rows in tiles:
        d_msg = mm(hot_d[rows, :], d_agg)
        d_edge = norm_back(d_msg * edge_gain, unit[rows, :], scale[rows, :])
        d_hid = mm_nt(d_edge.astype(BF16), w2[...]).astype(BF16).astype(F32)
        gp[rows, :] = (d_hid * slope[rows, :]).astype(BF16)
    copies[8].wait()
    gw[0:width, :] = mm_tn(edge[...], gp[...]).astype(BF16)
    sm = mm(hot_st[...], gp[...]).astype(BF16)
    gw[width : 2 * width, :] = mm_tn(table[...], sm).astype(BF16)
    sg = mm(hot_dt[...], gp[...]).astype(BF16)
    sg_ref[...] = sg
    gw[2 * width : 3 * width, :] = mm_tn(grid[...], sg).astype(BF16)
    core = parity("sector")
    half = width // 2
    piece = gw.shape[0] // (2 * len(piece_order()))
    for i, j in enumerate(piece_order()):
        rows = slice(i * piece, (i + 1) * piece)
        mine = pl.ds(pl.multiple_of((2 * j + core) * piece, piece), piece)
        other = pl.ds(pl.multiple_of((2 * j + 1 - core) * piece, piece), piece)
        send_a[rows, :] = gw[other, 0:half]
        send_b[rows, :] = gw[other, half:width]
        keep_a[rows, :] = gw[mine, 0:half]
        keep_b[rows, :] = gw[mine, half:width]
    grad_table = mm_nt(sm, wm[...])
    own_ref[...] = grad_table[0:own]
    borrowed[...] = grad_table[own:].astype(BF16)
    for start, out in zip(starts, (b0_ref, b1_ref, b2_ref, b3_ref)):
        out[...] = borrowed[pl.ds(start, margin), :]


def main(edge_src, edge_dst, mesh_lat, received, edge_gain, node_gain, base, node, edge_feat, grid_block, cot_block, w1, w2, n1, n2):
    edges, width = edge_feat.shape
    points = grid_block.shape[0]
    table = mesh_lat.shape[0] + 4 * received[0].shape[0]
    sds = jax.ShapeDtypeStruct
    square = pltpu.VMEM((width, width), BF16)
    nodes = pltpu.VMEM((points, width), BF16)
    return pl.pallas_call(
        main_kernel,
        out_shape=[
            sds((points, width), BF16),
            sds((points, width), BF16),
            sds((points, width), BF16),
            sds(mesh_lat.shape, F32),
        ]
        + [sds(received[0].shape, BF16)] * 4
        + [sds((3 * width // 2, width // 2), BF16)] * 4,
        in_specs=[VM] * 9 + [ANY] * 9,
        out_specs=[VM] * 12,
        scratch_shapes=[
            pltpu.VMEM((edges, width), F32),
            pltpu.VMEM((points, width), F32),
            pltpu.VMEM((edges, width), BF16),
            nodes,
            nodes,
            square,
            square,
            square,
            square,
            pltpu.VMEM((table, width), BF16),
            pltpu.VMEM((table, width), BF16),
            pltpu.VMEM((edges, table), BF16),
            pltpu.VMEM((edges, points), BF16),
            pltpu.VMEM((table, edges), BF16),
            pltpu.VMEM((points, edges), BF16),
            pltpu.VMEM((edges, width), F32),
            pltpu.VMEM((edges, width), F32),
            pltpu.VMEM((edges, 1), F32),
            pltpu.VMEM((edges, width), BF16),
            pltpu.VMEM((edges, width), BF16),
            pltpu.VMEM((3 * width, width), BF16),
            pltpu.VMEM((table - mesh_lat.shape[0], width), BF16),
            pltpu.SemaphoreType.DMA((9,)),
        ],
        compiler_params=pltpu.CompilerParams(vmem_limit_bytes=56 << 20),
        name="main",
        cost_estimate=pl.CostEstimate(
            flops=16 * edges * width * width,
            bytes_accessed=14 * edges * width,
            transcendentals=edges * width,
        ),
    )(
        edge_src.reshape(edges // LANES, LANES),
        edge_dst.reshape(edges // LANES, LANES),
        mesh_lat,
        *received,
        edge_gain.reshape(1, width),
        node_gain.reshape(1, width),
        base,
        node,
        edge_feat,
        grid_block,
        cot_block,
        w1,
        w2,
        n1,
        n2,
    )


def grid_kernel(sg_ref, w1_ref, dnpre_ref, n1_ref, cot_ref, out_ref):
    total = cot_ref[...].astype(F32) + mm_nt(dnpre_ref[...], n1_ref[...]) + mm_nt(sg_ref[...], w1_ref[...])
    out_ref[...] = total.astype(BF16)


def grid_grads(sg, w1, dnpre, n1, cot_block):
    points, width = sg.shape
    return pl.pallas_call(
        grid_kernel,
        out_shape=jax.ShapeDtypeStruct((points, width), BF16),
        in_specs=[VM, pl.BlockSpec((width, width), lambda k: (2, 0)), VM, pl.BlockSpec((width, width), lambda k: (1, 0)), VM],
        out_specs=VM,
        grid=(1,),
        name="grid_grads",
        cost_estimate=pl.CostEstimate(flops=4 * points * width * width, bytes_accessed=3 << 20, transcendentals=0),
    )(sg, w1, dnpre, n1, cot_block)


def mesh_kernel(send_ref, own_ref, r0_ref, r1_ref, r2_ref, r3_ref, out_ref, back):
    margin = r0_ref.shape[0]
    parts = (r0_ref, r1_ref, r2_ref, r3_ref)
    for pair, axis in enumerate(("sector", "band")):
        odd = parity(axis)
        for turn, group in enumerate((1 - odd, odd)):
            back[pl.ds(pl.multiple_of((2 * pair + group) * margin, margin), margin), :] = parts[2 * pair + turn][...]
    hot = onehot_rows(send_ref[...], own_ref.shape[0])
    out_ref[...] = (own_ref[...] + mm(hot, back[...])).astype(BF16)


def mesh_grads(send_rows, own, returned):
    n = send_rows.shape[0]
    return pl.pallas_call(
        mesh_kernel,
        out_shape=jax.ShapeDtypeStruct(own.shape, BF16),
        in_specs=[VM] * 6,
        out_specs=VM,
        scratch_shapes=[pltpu.VMEM((n, own.shape[1]), BF16)],
        name="mesh_grads",
        cost_estimate=pl.CostEstimate(flops=2 * n * n * own.shape[1], bytes_accessed=1 << 19, transcendentals=0),
    )(send_rows.reshape(1, n), own, *returned)


def swap(parts):
    sectors, bands = lax.axis_size("sector"), lax.axis_size("band")

    def pairs(first, count, devices):
        ups = [(i, (i + 1) % devices) for i in range(first, count, 2)]
        return ups + [(j, i) for i, j in ups]

    return [
        lax.ppermute(parts[0], "sector", pairs(0, sectors, sectors)),
        lax.ppermute(parts[1], "sector", pairs(1, sectors, sectors)),
        lax.ppermute(parts[2], "band", pairs(0, bands - 1, bands)),
        lax.ppermute(parts[3], "band", pairs(1, bands - 1, bands)),
    ]


def coordinates(band, sector):
    return {
        "x_lo": band // 4,
        "y": gray(band % 4),
        "x_hi": sector // 16,
        "z": gray(sector % 16 // 2),
        "core": sector % 2,
    }


def send(values, flips):
    place = {}
    for band in range(lax.axis_size("band")):
        for sector in range(lax.axis_size("sector")):
            place[tuple(coordinates(band, sector).values())] = band * lax.axis_size("sector") + sector
    names = list(coordinates(0, 0))
    pairs = []
    for spot, source in place.items():
        target = list(spot)
        for name, bit in flips:
            target[names.index(name)] ^= 1 << bit
        pairs.append((source, place[tuple(target)]))
    return lax.ppermute(values, ("band", "sector"), sorted(pairs))


def plus(a, b):
    return (a.astype(F32) + b.astype(F32)).astype(BF16)


def halve(low, high, bit, flip):
    return plus(jnp.where(bit, high, low), send(jnp.where(bit, low, high), [flip]))


def reduce_weights(send_a, send_b, keep_a, keep_b):
    here = coordinates(lax.axis_index("band"), lax.axis_index("sector"))

    def bit(name, k):
        return ((here[name] >> k) & 1) == 1

    def rows(values, name, k):
        n = values.shape[0] // 2
        return halve(values[:n], values[n:], bit(name, k), (name, k))

    def cols(values, name, k):
        n = values.shape[1] // 2
        return halve(values[:, :n], values[:, n:], bit(name, k), (name, k))

    part_a = plus(keep_a, send(send_a, [("core", 0)]))
    part_b = plus(keep_b, send(send_b, [("core", 0)]))
    part_a = cols(rows(part_a, "z", 0), "y", 0)
    part_b = rows(cols(part_b, "y", 0), "z", 0)
    part = halve(part_a, part_b, bit("x_lo", 0), ("x_lo", 0))
    part = rows(rows(part, "z", 1), "z", 2)
    part = rows(part, "x_hi", 0)
    part = plus(part, send(part, [("y", 1)]))
    by_y = send(part, [("y", 0)])
    by_x = send(part, [("x_lo", 0)])
    by_both = send(part, [("y", 0), ("x_lo", 0)])
    odd_y, odd_x = bit("y", 0), bit("x_lo", 0)

    def ordered(mine, other):
        return jnp.concatenate([jnp.where(odd_y, other, mine), jnp.where(odd_y, mine, other)], axis=1)

    near, far = ordered(part, by_y), ordered(by_x, by_both)
    return jnp.concatenate([jnp.where(odd_x, far, near), jnp.where(odd_x, near, far)], axis=1).astype(F32)


def shards(
    grid_lat,
    mesh_lat,
    edge_feat,
    edge_src,
    edge_dst,
    send_rows,
    w_edge1,
    w_edge2,
    edge_gain,
    w_node1,
    w_node2,
    node_gain,
    cotangent,
):
    lat_rows, lon_cols, width = grid_lat.shape
    grid_block = grid_lat.reshape(lat_rows * lon_cols, width)
    cot_block = cotangent.reshape(lat_rows * lon_cols, width)
    received = swap(pick(send_rows, mesh_lat))
    base, node = early(edge_dst, grid_block, edge_feat, w_edge1, w_node1)
    result, dnpre, sg, own_grad, *rest = main(
        edge_src, edge_dst, mesh_lat, received, edge_gain, node_gain, base, node, edge_feat, grid_block, cot_block, w_edge1, w_edge2, w_node1, w_node2
    )
    grad_w = reduce_weights(*rest[4:])
    returned = swap(rest[:4])
    grad_grid = grid_grads(sg, w_edge1, dnpre, w_node1, cot_block)
    grad_mesh = mesh_grads(send_rows, own_grad, returned)
    total_edges = edge_feat.shape[0] * lax.axis_size("band") * lax.axis_size("sector")
    grad_w = grad_w * (1.0 / math.sqrt(total_edges))
    return (
        result.reshape(lat_rows, lon_cols, width),
        grad_grid.reshape(lat_rows, lon_cols, width),
        grad_mesh,
        grad_w,
    )


def solution(mesh):
    rows = P(("band", "sector"), None)
    flat = P(("band", "sector"))
    grid = P("band", "sector", None)
    in_specs = (grid, rows, rows, flat, flat, flat, P(), P(), P(), P(), P(), P(), grid)
    out_specs = (grid, grid, rows, P("sector", None))
    return jax.shard_map(shards, mesh=mesh, in_specs=in_specs, out_specs=out_specs, check_vma=False)
```

```python
import math

import jax
import jax.numpy as jnp
from jax import lax
from jax.experimental import pallas as pl
from jax.experimental.pallas import tpu as pltpu
from jax.sharding import PartitionSpec as P

EPSILON = 1e-05
BF16 = jnp.bfloat16
F32 = jnp.float32
ANY = pl.BlockSpec(memory_space=pl.ANY)
VM = pl.BlockSpec(memory_space=pltpu.VMEM)


def mm(a, b):
    return lax.dot_general(a, b, (((1,), (0,)), ((), ())), preferred_element_type=F32)


def mm_nt(a, b):
    return lax.dot_general(a, b, (((1,), (1,)), ((), ())), preferred_element_type=F32)


def mm_tn(a, b):
    return lax.dot_general(a, b, (((0,), (0,)), ((), ())), preferred_element_type=F32)


def onehot_rows(index_row, rows):
    n = index_row.shape[1]
    return (lax.broadcasted_iota(jnp.int32, (rows, n), 0) == index_row).astype(BF16)


def onehot_cols(index_col, cols):
    n = index_col.shape[0]
    return (lax.broadcasted_iota(jnp.int32, (n, cols), 1) == index_col).astype(BF16)


LANES = 128


def fill_rows(index_ref, hot_ref):
    for j in range(index_ref.shape[0]):
        hot_ref[:, j * LANES : (j + 1) * LANES] = onehot_rows(index_ref[j : j + 1, :], hot_ref.shape[0])


def fill_cols(index_ref, hot_ref):
    turned = jnp.transpose(index_ref[...])
    for j in range(index_ref.shape[0]):
        hot_ref[j * LANES : (j + 1) * LANES, :] = onehot_cols(turned[:, j : j + 1], hot_ref.shape[1])


def swish_parts(pre):
    sig = 0.5 * jnp.tanh(0.5 * pre) + 0.5
    value = pre * sig
    return value, sig + value * (1.0 - sig)


def norm_parts(raw):
    width = raw.shape[1]
    centred = raw - jnp.sum(raw, axis=1, keepdims=True) * (1.0 / width)
    spread = jnp.sum(centred * centred, axis=1, keepdims=True) * (1.0 / width)
    scale = lax.rsqrt(spread + EPSILON)
    return centred * scale, scale


def norm_back(grad, unit, scale):
    width = grad.shape[1]
    first = jnp.sum(grad, axis=1, keepdims=True) * (1.0 / width)
    second = jnp.sum(grad * unit, axis=1, keepdims=True) * (1.0 / width)
    return (grad - first - unit * second) * scale


def parity(axis):
    return lax.axis_index(axis) % 2


def pick_kernel(send_ref, mesh_ref, *refs):
    outs, picked = refs[:4], refs[4]
    hot = onehot_rows(send_ref[...], mesh_ref.shape[0])
    picked[...] = mm_tn(hot, mesh_ref[...]).astype(BF16)
    margin = outs[0].shape[0]
    for pair, axis in enumerate(("sector", "band")):
        odd = parity(axis)
        for turn in range(2):
            group = 2 * pair + (1 - odd if turn == 0 else odd)
            outs[2 * pair + turn][...] = picked[pl.ds(pl.multiple_of(group * margin, margin), margin), :]


def pick(send_rows, mesh_lat):
    n, width = send_rows.shape[0], mesh_lat.shape[1]
    part = jax.ShapeDtypeStruct((n // 4, width), BF16)
    return pl.pallas_call(
        pick_kernel,
        out_shape=[part] * 4,
        in_specs=[VM, VM],
        out_specs=[VM] * 4,
        scratch_shapes=[pltpu.VMEM((n, width), BF16)],
        name="pick",
        cost_estimate=pl.CostEstimate(flops=2 * n * n * width, bytes_accessed=2 * n * width * 2, transcendentals=0),
    )(send_rows.reshape(1, n), mesh_lat)


TILE = 512


def gray(value):
    return value ^ (value >> 1)


def piece_order():
    pieces = []
    for block in range(16):
        code = (block >> 3) | ((block >> 2) & 1) << 1 | ((block >> 1) & 1) << 2
        z = next(i for i in range(8) if gray(i) == code)
        pieces.append((block & 1) * 8 + z)
    return pieces


def main_kernel(
    src_ref,
    dst_ref,
    mesh_ref,
    r0_ref,
    r1_ref,
    r2_ref,
    r3_ref,
    eg_ref,
    ng_ref,
    edge_hbm,
    grid_hbm,
    cot_hbm,
    w1_hbm,
    w2_hbm,
    n1_hbm,
    n2_hbm,
    out_ref,
    dnpre_ref,
    sg_ref,
    own_ref,
    b0_ref,
    b1_ref,
    b2_ref,
    b3_ref,
    send_a,
    send_b,
    keep_a,
    keep_b,
    edge,
    grid,
    cot,
    w1,
    w2,
    n1,
    n2,
    table,
    prod,
    prod_g,
    hot_s,
    hot_d,
    hot_st,
    hot_dt,
    slope,
    unit,
    scale,
    msg,
    gp,
    gw,
    borrowed,
    sems,
):
    width = w2.shape[0]
    edges, points, rows_table = edge.shape[0], grid.shape[0], table.shape[0]
    tiles = [slice(t * TILE, (t + 1) * TILE) for t in range(edges // TILE)]
    grid_copy, w1_copy, edge_copy, w2_copy, n1_copy, n2_copy, cot_copy = copies = [
        pltpu.make_async_copy(source, target, sems.at[i])
        for i, (source, target) in enumerate(
            ((grid_hbm, grid), (w1_hbm, w1), (edge_hbm, edge), (w2_hbm, w2), (n1_hbm, n1), (n2_hbm, n2), (cot_hbm, cot))
        )
    ]
    for copy in copies:
        copy.start()
    own, margin = mesh_ref.shape[0], r0_ref.shape[0]
    table[0:own, :] = mesh_ref[...]
    starts = []
    for pair, axis in enumerate(("sector", "band")):
        odd = parity(axis)
        for slot in (1 - odd, odd):
            starts.append(pl.multiple_of((2 * pair + slot) * margin, margin))
    for start, part in zip(starts, (r0_ref, r1_ref, r2_ref, r3_ref)):
        table[pl.ds(own + start, margin), :] = part[...]
    fill_cols(src_ref, hot_s)
    fill_cols(dst_ref, hot_d)
    fill_rows(src_ref, hot_st)
    fill_rows(dst_ref, hot_dt)
    edge_gain, node_gain = eg_ref[...], ng_ref[...]

    grid_copy.wait()
    w1_copy.wait()
    w_edge, w_mesh, w_grid = (w1.at[pl.ds(i * width, width), :] for i in range(3))
    prod[...] = mm(table[...], w_mesh[...]).astype(BF16)
    prod_g[...] = mm(grid[...], w_grid[...]).astype(BF16)
    edge_copy.wait()
    w2_copy.wait()
    for rows in tiles:
        pre = mm(edge[rows, :], w_edge[...]) + mm(hot_s[rows, :], prod[...]) + mm(hot_d[rows, :], prod_g[...])
        hidden, steep = swish_parts(pre)
        slope[rows, :] = steep
        normed, inv = norm_parts(mm(hidden.astype(BF16), w2[...]))
        unit[rows, :] = normed
        scale[rows, :] = inv
        msg[rows, :] = (normed * edge_gain).astype(BF16)
    for copy in (n1_copy, n2_copy, cot_copy):
        copy.wait()
    n1_agg, n1_grid = (n1.at[pl.ds(i * width, width), :] for i in range(2))
    agg = mm(hot_dt[...], msg[...]).astype(BF16)
    node_hidden, node_slope = swish_parts(mm(agg, n1_agg[...]) + mm(grid[...], n1_grid[...]))
    node_unit, node_inv = norm_parts(mm(node_hidden.astype(BF16), n2[...]))
    out_ref[...] = (grid[...].astype(F32) + node_unit * node_gain).astype(BF16)
    d_raw = norm_back(cot[...].astype(F32) * node_gain, node_unit, node_inv)
    d_hidden = mm_nt(d_raw.astype(BF16), n2[...]).astype(BF16).astype(F32)
    d_pre = (d_hidden * node_slope).astype(BF16)
    dnpre_ref[...] = d_pre
    d_agg = mm_nt(d_pre, n1_agg[...]).astype(BF16)
    for rows in tiles:
        d_msg = mm(hot_d[rows, :], d_agg)
        d_edge = norm_back(d_msg * edge_gain, unit[rows, :], scale[rows, :])
        d_hid = mm_nt(d_edge.astype(BF16), w2[...]).astype(BF16).astype(F32)
        gp[rows, :] = (d_hid * slope[rows, :]).astype(BF16)
    gw[0:width, :] = mm_tn(edge[...], gp[...]).astype(BF16)
    sm = mm(hot_st[...], gp[...]).astype(BF16)
    gw[width : 2 * width, :] = mm_tn(table[...], sm).astype(BF16)
    sg = mm(hot_dt[...], gp[...]).astype(BF16)
    sg_ref[...] = sg
    gw[2 * width : 3 * width, :] = mm_tn(grid[...], sg).astype(BF16)
    core = parity("sector")
    half = width // 2
    piece = gw.shape[0] // (2 * len(piece_order()))
    for i, j in enumerate(piece_order()):
        rows = slice(i * piece, (i + 1) * piece)
        mine = pl.ds(pl.multiple_of((2 * j + core) * piece, piece), piece)
        other = pl.ds(pl.multiple_of((2 * j + 1 - core) * piece, piece), piece)
        send_a[rows, :] = gw[other, 0:half]
        send_b[rows, :] = gw[other, half:width]
        keep_a[rows, :] = gw[mine, 0:half]
        keep_b[rows, :] = gw[mine, half:width]
    grad_table = mm_nt(sm, w_mesh[...])
    own_ref[...] = grad_table[0:own]
    borrowed[...] = grad_table[own:].astype(BF16)
    for start, out in zip(starts, (b0_ref, b1_ref, b2_ref, b3_ref)):
        out[...] = borrowed[pl.ds(start, margin), :]


def main(edge_src, edge_dst, mesh_lat, received, edge_gain, node_gain, edge_feat, grid_block, cot_block, w1, w2, n1, n2):
    edges, width = edge_feat.shape
    points = grid_block.shape[0]
    table = mesh_lat.shape[0] + 4 * received[0].shape[0]
    sds = jax.ShapeDtypeStruct
    square = pltpu.VMEM((width, width), BF16)
    nodes = pltpu.VMEM((points, width), BF16)
    return pl.pallas_call(
        main_kernel,
        out_shape=[
            sds((points, width), BF16),
            sds((points, width), BF16),
            sds((points, width), BF16),
            sds(mesh_lat.shape, F32),
        ]
        + [sds(received[0].shape, BF16)] * 4
        + [sds((3 * width // 2, width // 2), BF16)] * 4,
        in_specs=[VM] * 9 + [ANY] * 7,
        out_specs=[VM] * 12,
        scratch_shapes=[
            pltpu.VMEM((edges, width), BF16),
            nodes,
            nodes,
            pltpu.VMEM(w1.shape, BF16),
            square,
            pltpu.VMEM(n1.shape, BF16),
            square,
            pltpu.VMEM((table, width), BF16),
            pltpu.VMEM((table, width), BF16),
            nodes,
            pltpu.VMEM((edges, table), BF16),
            pltpu.VMEM((edges, points), BF16),
            pltpu.VMEM((table, edges), BF16),
            pltpu.VMEM((points, edges), BF16),
            pltpu.VMEM((edges, width), F32),
            pltpu.VMEM((edges, width), F32),
            pltpu.VMEM((edges, 1), F32),
            pltpu.VMEM((edges, width), BF16),
            pltpu.VMEM((edges, width), BF16),
            pltpu.VMEM((3 * width, width), BF16),
            pltpu.VMEM((table - mesh_lat.shape[0], width), BF16),
            pltpu.SemaphoreType.DMA((7,)),
        ],
        compiler_params=pltpu.CompilerParams(vmem_limit_bytes=56 << 20),
        name="main",
        cost_estimate=pl.CostEstimate(
            flops=22 * edges * width * width,
            bytes_accessed=14 * edges * width,
            transcendentals=edges * width,
        ),
    )(
        edge_src.reshape(edges // LANES, LANES),
        edge_dst.reshape(edges // LANES, LANES),
        mesh_lat,
        *received,
        edge_gain.reshape(1, width),
        node_gain.reshape(1, width),
        edge_feat,
        grid_block,
        cot_block,
        w1,
        w2,
        n1,
        n2,
    )


def grid_kernel(sg_ref, w1_ref, dnpre_ref, n1_ref, cot_ref, out_ref):
    total = cot_ref[...].astype(F32) + mm_nt(dnpre_ref[...], n1_ref[...]) + mm_nt(sg_ref[...], w1_ref[...])
    out_ref[...] = total.astype(BF16)


def grid_grads(sg, w1, dnpre, n1, cot_block):
    points, width = sg.shape
    return pl.pallas_call(
        grid_kernel,
        out_shape=jax.ShapeDtypeStruct((points, width), BF16),
        in_specs=[VM, pl.BlockSpec((width, width), lambda k: (2, 0)), VM, pl.BlockSpec((width, width), lambda k: (1, 0)), VM],
        out_specs=VM,
        grid=(1,),
        name="grid_grads",
        cost_estimate=pl.CostEstimate(flops=4 * points * width * width, bytes_accessed=3 << 20, transcendentals=0),
    )(sg, w1, dnpre, n1, cot_block)


def mesh_kernel(send_ref, own_ref, r0_ref, r1_ref, r2_ref, r3_ref, out_ref, back):
    margin = r0_ref.shape[0]
    parts = (r0_ref, r1_ref, r2_ref, r3_ref)
    for pair, axis in enumerate(("sector", "band")):
        odd = parity(axis)
        for turn, group in enumerate((1 - odd, odd)):
            back[pl.ds(pl.multiple_of((2 * pair + group) * margin, margin), margin), :] = parts[2 * pair + turn][...]
    hot = onehot_rows(send_ref[...], own_ref.shape[0])
    out_ref[...] = (own_ref[...] + mm(hot, back[...])).astype(BF16)


def mesh_grads(send_rows, own, returned):
    n = send_rows.shape[0]
    return pl.pallas_call(
        mesh_kernel,
        out_shape=jax.ShapeDtypeStruct(own.shape, BF16),
        in_specs=[VM] * 6,
        out_specs=VM,
        scratch_shapes=[pltpu.VMEM((n, own.shape[1]), BF16)],
        name="mesh_grads",
        cost_estimate=pl.CostEstimate(flops=2 * n * n * own.shape[1], bytes_accessed=1 << 19, transcendentals=0),
    )(send_rows.reshape(1, n), own, *returned)


def swap(parts):
    sectors, bands = lax.axis_size("sector"), lax.axis_size("band")

    def pairs(first, count, devices):
        ups = [(i, (i + 1) % devices) for i in range(first, count, 2)]
        return ups + [(j, i) for i, j in ups]

    return [
        lax.ppermute(parts[0], "sector", pairs(0, sectors, sectors)),
        lax.ppermute(parts[1], "sector", pairs(1, sectors, sectors)),
        lax.ppermute(parts[2], "band", pairs(0, bands - 1, bands)),
        lax.ppermute(parts[3], "band", pairs(1, bands - 1, bands)),
    ]


def coordinates(band, sector):
    return {
        "x_lo": band // 4,
        "y": gray(band % 4),
        "x_hi": sector // 16,
        "z": gray(sector % 16 // 2),
        "core": sector % 2,
    }


def send(values, flips):
    place = {}
    for band in range(lax.axis_size("band")):
        for sector in range(lax.axis_size("sector")):
            place[tuple(coordinates(band, sector).values())] = band * lax.axis_size("sector") + sector
    names = list(coordinates(0, 0))
    pairs = []
    for spot, source in place.items():
        target = list(spot)
        for name, bit in flips:
            target[names.index(name)] ^= 1 << bit
        pairs.append((source, place[tuple(target)]))
    return lax.ppermute(values, ("band", "sector"), sorted(pairs))


def total(*terms):
    return sum(term.astype(F32) for term in terms).astype(BF16)


def plus(a, b):
    return total(a, b)


def reduce_weights(send_a, send_b, keep_a, keep_b, tails):
    here = coordinates(lax.axis_index("band"), lax.axis_index("sector"))

    def bit(name, k=0):
        return ((here[name] >> k) & 1) == 1

    def halve(low, high, name, k=0):
        mine = bit(name, k)
        return jnp.where(mine, high, low), send(jnp.where(mine, low, high), [(name, k)])

    def quarter(values, first, second):
        parts = values.reshape(2, 2, values.shape[0] // 4, values.shape[1])
        one, two = bit(*first), bit(*second)

        def part(swap_one, swap_two):
            low, high = (jnp.where(two != swap_two, row[1], row[0]) for row in parts)
            return jnp.where(one != swap_one, high, low)

        return part(False, False), send(part(True, False), [first]), send(part(False, True), [second]), send(part(True, True), [first, second])

    def halves(values, axis):
        return jnp.split(values, 2, axis=axis)

    part_a = plus(keep_a, send(send_a, [("core", 0)]))
    part_b = plus(keep_b, send(send_b, [("core", 0)]))
    a, got_a = halve(*halves(part_a, 0), "z")
    b, got_b = halve(*halves(part_b, 1), "y")
    got_a, got_b = tails[0](got_a, got_b)
    a, got_a = halve(*halves(plus(a, got_a), 1), "y")
    b, got_b = halve(*halves(plus(b, got_b), 0), "z")
    got_a, got_b = tails[1](got_a, got_b)
    both = jnp.stack([plus(a, got_a).reshape(2, -1, a.shape[1]), plus(b, got_b).reshape(2, -1, a.shape[1])])
    held, *got = quarter(both.reshape(-1, a.shape[1]), ("x_lo", 0), ("z", 1))
    got = tails[2](*got)
    part = total(held, *got)
    held, *got = quarter(part, ("z", 2), ("x_hi", 0))
    got = tails[3](*got)
    part = total(held, *got)
    part = plus(part, send(part, [("y", 1)]))
    by_y = send(part, [("y", 0)])
    by_x = send(part, [("x_lo", 0)])
    by_both = send(part, [("y", 0), ("x_lo", 0)])
    odd_y, odd_x = bit("y"), bit("x_lo")

    def ordered(mine, other):
        return jnp.concatenate([jnp.where(odd_y, other, mine), jnp.where(odd_y, mine, other)], axis=1)

    near, far = ordered(part, by_y), ordered(by_x, by_both)
    return jnp.concatenate([jnp.where(odd_x, far, near), jnp.where(odd_x, near, far)], axis=1).astype(F32)


def shards(
    grid_lat,
    mesh_lat,
    edge_feat,
    edge_src,
    edge_dst,
    send_rows,
    w_edge1,
    w_edge2,
    edge_gain,
    w_node1,
    w_node2,
    node_gain,
    cotangent,
):
    lat_rows, lon_cols, width = grid_lat.shape
    grid_block = grid_lat.reshape(lat_rows * lon_cols, width)
    cot_block = cotangent.reshape(lat_rows * lon_cols, width)
    received = swap(pick(send_rows, mesh_lat))
    result, dnpre, sg, own_grad, *rest = main(
        edge_src, edge_dst, mesh_lat, received, edge_gain, node_gain, edge_feat, grid_block, cot_block, w_edge1, w_edge2, w_node1, w_node2
    )
    done = {}

    def after_first(*got):
        done["grid"], *got = lax.optimization_barrier((grid_grads(sg, w_edge1, dnpre, w_node1, cot_block), *got))
        return got

    def after_second(*got):
        return got

    def after_third(*got):
        *parts, first = lax.optimization_barrier((*rest[:4], got[0]))
        done["returned"] = swap(parts)
        return (first, *got[1:])

    def after_fourth(*got):
        done["mesh"], *got = lax.optimization_barrier((mesh_grads(send_rows, own_grad, done["returned"]), *got))
        return got

    grad_w = reduce_weights(*rest[4:], (after_first, after_second, after_third, after_fourth))
    total_edges = edge_feat.shape[0] * lax.axis_size("band") * lax.axis_size("sector")
    grad_w = grad_w * (1.0 / math.sqrt(total_edges))
    return (
        result.reshape(lat_rows, lon_cols, width),
        done["grid"].reshape(lat_rows, lon_cols, width),
        done["mesh"],
        grad_w,
    )


def solution(mesh):
    rows = P(("band", "sector"), None)
    flat = P(("band", "sector"))
    grid = P("band", "sector", None)
    in_specs = (grid, rows, rows, flat, flat, flat, P(), P(), P(), P(), P(), P(), grid)
    out_specs = (grid, grid, rows, P("sector", None))
    return jax.shard_map(shards, mesh=mesh, in_specs=in_specs, out_specs=out_specs, check_vma=False)
```

```python
import math

import jax
import jax.numpy as jnp
from jax import lax
from jax.experimental import pallas as pl
from jax.experimental.pallas import tpu as pltpu
from jax.sharding import PartitionSpec as P

EPSILON = 1e-05
BF16 = jnp.bfloat16
F32 = jnp.float32
ANY = pl.BlockSpec(memory_space=pl.ANY)
VM = pl.BlockSpec(memory_space=pltpu.VMEM)


def mm(a, b):
    return lax.dot_general(a, b, (((1,), (0,)), ((), ())), preferred_element_type=F32)


def mm_nt(a, b):
    return lax.dot_general(a, b, (((1,), (1,)), ((), ())), preferred_element_type=F32)


def mm_tn(a, b):
    return lax.dot_general(a, b, (((0,), (0,)), ((), ())), preferred_element_type=F32)


def onehot_rows(index_row, rows):
    n = index_row.shape[1]
    return (lax.broadcasted_iota(jnp.int32, (rows, n), 0) == index_row).astype(BF16)


def onehot_cols(index_col, cols):
    n = index_col.shape[0]
    return (lax.broadcasted_iota(jnp.int32, (n, cols), 1) == index_col).astype(BF16)


LANES = 128


def fill_rows(index_ref, hot_ref):
    for j in range(index_ref.shape[0]):
        hot_ref[:, j * LANES : (j + 1) * LANES] = onehot_rows(index_ref[j : j + 1, :], hot_ref.shape[0])


def fill_cols(index_ref, hot_ref):
    turned = jnp.transpose(index_ref[...])
    for j in range(index_ref.shape[0]):
        hot_ref[j * LANES : (j + 1) * LANES, :] = onehot_cols(turned[:, j : j + 1], hot_ref.shape[1])


def swish_parts(pre):
    sig = 0.5 * jnp.tanh(0.5 * pre) + 0.5
    value = pre * sig
    return value, sig + value * (1.0 - sig)


def norm_parts(raw):
    width = raw.shape[1]
    centred = raw - jnp.sum(raw, axis=1, keepdims=True) * (1.0 / width)
    spread = jnp.sum(centred * centred, axis=1, keepdims=True) * (1.0 / width)
    scale = lax.rsqrt(spread + EPSILON)
    return centred * scale, scale


def norm_back(grad, unit, scale):
    width = grad.shape[1]
    first = jnp.sum(grad, axis=1, keepdims=True) * (1.0 / width)
    second = jnp.sum(grad * unit, axis=1, keepdims=True) * (1.0 / width)
    return (grad - first - unit * second) * scale


def parity(axis):
    return lax.axis_index(axis) % 2


def pick_kernel(send_ref, mesh_ref, *refs):
    outs, picked = refs[:4], refs[4]
    hot = onehot_rows(send_ref[...], mesh_ref.shape[0])
    picked[...] = mm_tn(hot, mesh_ref[...]).astype(BF16)
    margin = outs[0].shape[0]
    for pair, axis in enumerate(("sector", "band")):
        odd = parity(axis)
        for turn in range(2):
            group = 2 * pair + (1 - odd if turn == 0 else odd)
            outs[2 * pair + turn][...] = picked[pl.ds(pl.multiple_of(group * margin, margin), margin), :]


def pick(send_rows, mesh_lat):
    n, width = send_rows.shape[0], mesh_lat.shape[1]
    part = jax.ShapeDtypeStruct((n // 4, width), BF16)
    return pl.pallas_call(
        pick_kernel,
        out_shape=[part] * 4,
        in_specs=[VM, VM],
        out_specs=[VM] * 4,
        scratch_shapes=[pltpu.VMEM((n, width), BF16)],
        name="pick",
        cost_estimate=pl.CostEstimate(flops=2 * n * n * width, bytes_accessed=2 * n * width * 2, transcendentals=0),
    )(send_rows.reshape(1, n), mesh_lat)


TILE = 512


def gray(value):
    return value ^ (value >> 1)


def z_code(z):
    return z ^ (3 * (z >> 2))


def piece_order():
    pieces = []
    for block in range(16):
        code = (block >> 3) | ((block >> 2) & 1) << 1 | ((block >> 1) & 1) << 2
        z = next(i for i in range(8) if z_code(i) == code)
        pieces.append((block & 1) * 8 + z)
    return pieces


NODE_TILE = 512


def main_kernel(*refs):
    (src_hbm, dst_hbm, mesh_hbm, r0_hbm, r1_hbm, r2_hbm, r3_hbm, eg_hbm, ng_hbm), refs = refs[:9], refs[9:]
    (edge_hbm, grid_hbm, cot_hbm, w1_hbm, w2_hbm, n1_hbm, n2_hbm), refs = refs[:7], refs[7:]
    (out_hbm, gg_hbm, own_hbm, far_s_hbm, near_b_hbm, far_b_hbm, sa_hbm, sb_hbm, ka_hbm, kb_hbm), refs = refs[:10], refs[10:]
    (src, dst, parts, eg, ng, edge, grid, cot, w1, w2, n1, n2), refs = refs[:12], refs[12:]
    (out, gg, own_grad, far_s, near_b, far_b, send_a, send_b, keep_a, keep_b), refs = refs[:10], refs[10:]
    table, prod, prod_g, hot_s, hot_d, hot_st, hot_dt, slope, unit, scale, msg, gp, d_pre, gw, borrowed, sems, out_sems = refs

    width = w2.shape[0]
    edges, points, rows_table = edge.shape[0], grid.shape[0], table.shape[0]
    own, margin = mesh_hbm.shape[0], r0_hbm.shape[0]
    tiles = [slice(t * TILE, (t + 1) * TILE) for t in range(edges // TILE)]
    nodes = [slice(t * NODE_TILE, (t + 1) * NODE_TILE) for t in range(points // NODE_TILE)]
    received = [parts.at[pl.ds(i * margin, margin), :] for i in range(4)]
    pairs = (
        (dst_hbm, dst),
        (src_hbm, src),
        (grid_hbm, grid),
        (w1_hbm, w1),
        (edge_hbm, edge),
        (mesh_hbm, table.at[pl.ds(0, own), :]),
        (r0_hbm, received[0]),
        (r1_hbm, received[1]),
        (r2_hbm, received[2]),
        (r3_hbm, received[3]),
        (w2_hbm, w2),
        (eg_hbm, eg),
        (n1_hbm, n1),
        (ng_hbm, ng),
        (n2_hbm, n2),
        (cot_hbm, cot),
    )
    copies = [pltpu.make_async_copy(source, target, sems.at[i]) for i, (source, target) in enumerate(pairs)]
    for copy in copies:
        copy.start()

    results = (
        (out, out_hbm),
        (send_a, sa_hbm),
        (send_b, sb_hbm),
        (keep_a, ka_hbm),
        (keep_b, kb_hbm),
        (near_b, near_b_hbm),
        (far_s, far_s_hbm),
        (far_b, far_b_hbm),
        (own_grad, own_hbm),
        (gg, gg_hbm),
    )
    stores = [pltpu.make_async_copy(source, target, out_sems.at[i]) for i, (source, target) in enumerate(results)]

    copies[0].wait()
    fill_cols(dst, hot_d)
    fill_rows(dst, hot_dt)
    copies[1].wait()
    fill_cols(src, hot_s)
    fill_rows(src, hot_st)
    starts = []
    for pair, axis in enumerate(("sector", "band")):
        odd = parity(axis)
        for slot in (1 - odd, odd):
            starts.append(pl.multiple_of((2 * pair + slot) * margin, margin))
    copies[2].wait()
    copies[3].wait()
    w_edge, w_mesh, w_grid = (w1.at[pl.ds(i * width, width), :] for i in range(3))
    prod_g[...] = mm(grid[...], w_grid[...]).astype(BF16)
    for copy in copies[5:10]:
        copy.wait()
    for start, part in zip(starts, received):
        table[pl.ds(own + start, margin), :] = part[...]
    prod[...] = mm(table[...], w_mesh[...]).astype(BF16)
    copies[4].wait()
    copies[10].wait()
    copies[11].wait()
    edge_gain = eg[...]
    for rows in tiles:
        pre = mm(edge[rows, :], w_edge[...]) + mm(hot_s[rows, :], prod[...]) + mm(hot_d[rows, :], prod_g[...])
        hidden, steep = swish_parts(pre)
        slope[rows, :] = steep
        normed, inv = norm_parts(mm(hidden.astype(BF16), w2[...]))
        unit[rows, :] = normed
        scale[rows, :] = inv
        msg[rows, :] = (normed * edge_gain).astype(BF16)
    for copy in copies[12:]:
        copy.wait()
    node_gain = ng[...]
    n1_agg, n1_grid = (n1.at[pl.ds(i * width, width), :] for i in range(2))
    d_agg = []
    for rows in nodes:
        agg = mm(hot_dt[rows, :], msg[...]).astype(BF16)
        node_hidden, node_slope = swish_parts(mm(agg, n1_agg[...]) + mm(grid[rows, :], n1_grid[...]))
        node_unit, node_inv = norm_parts(mm(node_hidden.astype(BF16), n2[...]))
        out[rows, :] = (grid[rows, :].astype(F32) + node_unit * node_gain).astype(BF16)
        d_raw = norm_back(cot[rows, :].astype(F32) * node_gain, node_unit, node_inv)
        d_hidden = mm_nt(d_raw.astype(BF16), n2[...]).astype(BF16).astype(F32)
        d_pre[rows, :] = (d_hidden * node_slope).astype(BF16)
        d_agg.append(mm_nt(d_pre[rows, :], n1_agg[...]).astype(BF16))
    stores[0].start()
    d_agg = jnp.concatenate(d_agg, axis=0)
    for rows in tiles:
        d_msg = mm(hot_d[rows, :], d_agg)
        d_edge = norm_back(d_msg * edge_gain, unit[rows, :], scale[rows, :])
        d_hid = mm_nt(d_edge.astype(BF16), w2[...]).astype(BF16).astype(F32)
        gp[rows, :] = (d_hid * slope[rows, :]).astype(BF16)
    sm = mm(hot_st[...], gp[...]).astype(BF16)
    sg = mm(hot_dt[...], gp[...]).astype(BF16)
    gw[width : 2 * width, :] = mm_tn(table[...], sm).astype(BF16)
    grad_table = mm_nt(sm, w_mesh[...])
    gw[2 * width : 3 * width, :] = mm_tn(grid[...], sg).astype(BF16)
    gw[0:width, :] = mm_tn(edge[...], gp[...]).astype(BF16)
    core = parity("sector")
    half, quarter = width // 2, width // 4
    own_grad[...] = grad_table[0:own]
    borrowed[...] = grad_table[own:].astype(BF16)
    near_s_rows, far_s_rows, near_b_rows, far_b_rows = (borrowed[pl.ds(start, margin), :] for start in starts)
    kept = keep_a.shape[0]
    for i in range(2):
        send_a[kept + i * margin : kept + (i + 1) * margin, :] = near_s_rows[:, i * half : (i + 1) * half]
    for i in range(4):
        near_b[i * margin : (i + 1) * margin, :] = near_b_rows[:, i * quarter : (i + 1) * quarter]
    far_s[...] = far_s_rows
    far_b[...] = far_b_rows
    piece = gw.shape[0] // (2 * len(piece_order()))
    for i, j in enumerate(piece_order()):
        rows = slice(i * piece, (i + 1) * piece)
        mine = pl.ds(pl.multiple_of((2 * j + core) * piece, piece), piece)
        other = pl.ds(pl.multiple_of((2 * j + 1 - core) * piece, piece), piece)
        send_a[rows, :] = gw[other, 0:half]
        send_b[rows, :] = gw[other, half:width]
        keep_a[rows, :] = gw[mine, 0:half]
        keep_b[rows, :] = gw[mine, half:width]
    for store in stores[1:9]:
        store.start()
    gg[...] = (cot[...].astype(F32) + mm_nt(d_pre[...], n1_grid[...]) + mm_nt(sg, w_grid[...])).astype(BF16)
    stores[9].start()
    for store in stores:
        store.wait()


def main(edge_src, edge_dst, mesh_lat, received, edge_gain, node_gain, edge_feat, grid_block, cot_block, w1, w2, n1, n2):
    edges, width = edge_feat.shape
    points, own = grid_block.shape[0], mesh_lat.shape[0]
    margin = received[0].shape[0]
    table = own + 4 * margin
    half, quarter, kept = width // 2, width // 4, 3 * width // 2
    operands = (
        edge_src.reshape(edges // LANES, LANES),
        edge_dst.reshape(edges // LANES, LANES),
        mesh_lat,
        *received,
        edge_gain.reshape(1, width),
        node_gain.reshape(1, width),
        edge_feat,
        grid_block,
        cot_block,
        w1,
        w2,
        n1,
        n2,
    )
    outs = [
        ((points, width), BF16),
        ((points, width), BF16),
        ((own, width), F32),
        ((margin, width), BF16),
        ((4 * margin, quarter), BF16),
        ((margin, width), BF16),
        ((kept + 2 * margin, half), BF16),
        ((kept, half), BF16),
        ((kept, half), BF16),
        ((kept, half), BF16),
    ]
    local = [pltpu.VMEM(x.shape, x.dtype) for x in operands]
    scratch = [
        ((table, width), BF16),
        ((table, width), BF16),
        ((points, width), BF16),
        ((edges, table), BF16),
        ((edges, points), BF16),
        ((table, edges), BF16),
        ((points, edges), BF16),
        ((edges, width), F32),
        ((edges, width), F32),
        ((edges, 1), F32),
        ((edges, width), BF16),
        ((edges, width), BF16),
        ((points, width), BF16),
        ((3 * width, width), BF16),
        ((4 * margin, width), BF16),
    ]
    return pl.pallas_call(
        main_kernel,
        out_shape=[jax.ShapeDtypeStruct(*shape) for shape in outs],
        in_specs=[ANY] * len(operands),
        out_specs=[ANY] * len(outs),
        scratch_shapes=local[:2]
        + [pltpu.VMEM((4 * margin, width), BF16)]
        + local[7:]
        + [pltpu.VMEM(*shape) for shape in outs + scratch]
        + [pltpu.SemaphoreType.DMA((len(operands),)), pltpu.SemaphoreType.DMA((len(outs),))],
        compiler_params=pltpu.CompilerParams(vmem_limit_bytes=58 << 20),
        name="main",
        cost_estimate=pl.CostEstimate(
            flops=24 * edges * width * width,
            bytes_accessed=12 * edges * width,
            transcendentals=edges * width,
        ),
    )(*operands)


def mesh_kernel(send_ref, own_ref, near_s_ref, far_s_ref, near_b_ref, far_b_ref, out_ref, back):
    margin = far_s_ref.shape[0]
    width = far_s_ref.shape[1]
    for pair, (near, far) in enumerate(((near_s_ref, far_s_ref), (near_b_ref, far_b_ref))):
        odd = parity("band" if pair else "sector")
        first = pl.ds(pl.multiple_of((2 * pair + 1 - odd) * margin, margin), margin)
        second = pl.ds(pl.multiple_of((2 * pair + odd) * margin, margin), margin)
        for i in range(width // near.shape[1]):
            back[first, i * near.shape[1] : (i + 1) * near.shape[1]] = near[i * margin : (i + 1) * margin, :]
        back[second, :] = far[...]
    hot = onehot_rows(send_ref[...], own_ref.shape[0])
    out_ref[...] = (own_ref[...] + mm(hot, back[...])).astype(BF16)


def mesh_grads(send_rows, own, returned):
    n = send_rows.shape[0]
    return pl.pallas_call(
        mesh_kernel,
        out_shape=jax.ShapeDtypeStruct(own.shape, BF16),
        in_specs=[VM] * 6,
        out_specs=VM,
        scratch_shapes=[pltpu.VMEM((n, own.shape[1]), BF16)],
        name="mesh_grads",
        cost_estimate=pl.CostEstimate(flops=2 * n * n * own.shape[1], bytes_accessed=1 << 19, transcendentals=0),
    )(send_rows.reshape(1, n), own, *returned)


def trade(part, axis, turn):
    devices = lax.axis_size(axis)
    last = devices if axis == "sector" else devices - 1
    ups = [(i, (i + 1) % devices) for i in range(turn, last, 2)]
    return lax.ppermute(part, axis, ups + [(j, i) for i, j in ups])


def swap(parts):
    return [trade(parts[2 * pair + turn], axis, turn) for pair, axis in enumerate(("sector", "band")) for turn in range(2)]


def coordinates(band, sector):
    return {
        "x_lo": band // 4,
        "y": gray(band % 4),
        "x_hi": sector // 16,
        "z": z_code(sector % 16 // 2),
        "core": sector % 2,
    }


def send(values, flips):
    place = {}
    for band in range(lax.axis_size("band")):
        for sector in range(lax.axis_size("sector")):
            place[tuple(coordinates(band, sector).values())] = band * lax.axis_size("sector") + sector
    names = list(coordinates(0, 0))
    pairs = []
    for spot, source in place.items():
        target = list(spot)
        for name, bit in flips:
            target[names.index(name)] ^= 1 << bit
        pairs.append((source, place[tuple(target)]))
    return lax.ppermute(values, ("band", "sector"), sorted(pairs))


def total(*terms):
    return sum(term.astype(F32) for term in terms).astype(BF16)


def plus(a, b):
    return total(a, b)


def reduce_weights(near_b, send_a, send_b, keep_a, keep_b, tails):
    here = coordinates(lax.axis_index("band"), lax.axis_index("sector"))

    def bit(name, k=0):
        return ((here[name] >> k) & 1) == 1

    def halve(low, high, name, k=0):
        mine = bit(name, k)
        return jnp.where(mine, high, low), send(jnp.where(mine, low, high), [(name, k)])

    def quarter(values, first, second):
        parts = values.reshape(2, 2, values.shape[0] // 4, values.shape[1])
        one, two = bit(*first), bit(*second)

        def part(swap_one, swap_two):
            low, high = (jnp.where(two != swap_two, row[1], row[0]) for row in parts)
            return jnp.where(one != swap_one, high, low)

        return part(False, False), send(part(True, False), [first]), send(part(False, True), [second]), send(part(True, True), [first, second])

    def halves(values, axis):
        return jnp.split(values, 2, axis=axis)

    got_a = send(send_a, [("core", 0)])
    near_s = got_a[keep_a.shape[0] :]
    part_a = plus(keep_a, got_a[: keep_a.shape[0]])
    part_b = plus(keep_b, send(send_b, [("core", 0)]))
    a, got_a = halve(*halves(part_a, 0), "z")
    left, right = halves(part_b, 1)
    mine = bit("y")
    b = jnp.where(mine, right, left)
    got_b = send(jnp.concatenate([jnp.where(mine, left, right), near_b], axis=0), [("y", 0)])
    got_b, near_b = got_b[: b.shape[0]], got_b[b.shape[0] :]
    got_a, got_b = tails[0](part_b, got_a, got_b, near_s, near_b)
    a, got_a = halve(*halves(plus(a, got_a), 1), "y")
    b, got_b = halve(*halves(plus(b, got_b), 0), "z")
    got_a, got_b = tails[1](got_a, got_b)
    both = jnp.stack([plus(a, got_a).reshape(2, -1, a.shape[1]), plus(b, got_b).reshape(2, -1, a.shape[1])])
    held, *got = quarter(both.reshape(-1, a.shape[1]), ("x_lo", 0), ("z", 1))
    got = tails[2](*got)
    part = total(held, *got)
    held, *got = quarter(part, ("z", 2), ("x_hi", 0))
    got = tails[3](*got)
    part = total(held, *got)
    part = plus(part, send(part, [("y", 1)]))
    by_y = send(part, [("y", 0)])
    by_x = send(part, [("x_lo", 0)])
    by_both = send(part, [("y", 0), ("x_lo", 0)])
    odd_y, odd_x = bit("y"), bit("x_lo")

    def ordered(mine, other):
        return jnp.concatenate([jnp.where(odd_y, other, mine), jnp.where(odd_y, mine, other)], axis=1)

    near, far = ordered(part, by_y), ordered(by_x, by_both)
    return jnp.concatenate([jnp.where(odd_x, far, near), jnp.where(odd_x, near, far)], axis=1).astype(F32)


def shards(
    grid_lat,
    mesh_lat,
    edge_feat,
    edge_src,
    edge_dst,
    send_rows,
    w_edge1,
    w_edge2,
    edge_gain,
    w_node1,
    w_node2,
    node_gain,
    cotangent,
):
    lat_rows, lon_cols, width = grid_lat.shape
    grid_block = grid_lat.reshape(lat_rows * lon_cols, width)
    cot_block = cotangent.reshape(lat_rows * lon_cols, width)
    received = swap(pick(send_rows, mesh_lat))
    result, grad_grid, own_grad, far_s, near_b, far_b, *sums = main(
        edge_src, edge_dst, mesh_lat, received, edge_gain, node_gain, edge_feat, grid_block, cot_block, w_edge1, w_edge2, w_node1, w_node2
    )
    done = {}

    def after_first(part, got_a, got_b, near_s, near_b):
        far, _ = lax.optimization_barrier((far_s, part))
        far = trade(far, "sector", 1)
        done["near"] = near_s, near_b
        done["far_s"], *got = lax.optimization_barrier((far, got_a, got_b))
        done["first"] = got[0]
        return got

    def after_second(got_a, got_b):
        far, _ = lax.optimization_barrier((far_b, done["first"]))
        far = trade(far, "band", 1)
        done["far_b"], *got = lax.optimization_barrier((far, got_a, got_b))
        return got

    def after_third(*got):
        return got

    def after_fourth(*got):
        near_s, near_b = done["near"]
        grads = mesh_grads(send_rows, own_grad, (near_s, done["far_s"], near_b, done["far_b"]))
        done["mesh"], *got = lax.optimization_barrier((grads, *got))
        return got

    grad_w = reduce_weights(near_b, *sums, (after_first, after_second, after_third, after_fourth))
    total_edges = edge_feat.shape[0] * lax.axis_size("band") * lax.axis_size("sector")
    grad_w = grad_w * (1.0 / math.sqrt(total_edges))
    return (
        result.reshape(lat_rows, lon_cols, width),
        grad_grid.reshape(lat_rows, lon_cols, width),
        done["mesh"],
        grad_w,
    )


def solution(mesh):
    rows = P(("band", "sector"), None)
    flat = P(("band", "sector"))
    grid = P("band", "sector", None)
    in_specs = (grid, rows, rows, flat, flat, flat, P(), P(), P(), P(), P(), P(), grid)
    out_specs = (grid, grid, rows, P("sector", None))
    return jax.shard_map(shards, mesh=mesh, in_specs=in_specs, out_specs=out_specs, check_vma=False)
```

```python
import math

import jax
import jax.numpy as jnp
from jax import lax
from jax.experimental import pallas as pl
from jax.experimental.pallas import tpu as pltpu
from jax.sharding import PartitionSpec as P

EPSILON = 1e-05
BF16 = jnp.bfloat16
F32 = jnp.float32
ANY = pl.BlockSpec(memory_space=pl.ANY)
VM = pl.BlockSpec(memory_space=pltpu.VMEM)


def mm(a, b):
    return lax.dot_general(a, b, (((1,), (0,)), ((), ())), preferred_element_type=F32)


def mm_nt(a, b):
    return lax.dot_general(a, b, (((1,), (1,)), ((), ())), preferred_element_type=F32)


def mm_tn(a, b):
    return lax.dot_general(a, b, (((0,), (0,)), ((), ())), preferred_element_type=F32)


def onehot_rows(index_row, rows):
    n = index_row.shape[1]
    return (lax.broadcasted_iota(jnp.int32, (rows, n), 0) == index_row).astype(BF16)


def onehot_cols(index_col, cols):
    n = index_col.shape[0]
    return (lax.broadcasted_iota(jnp.int32, (n, cols), 1) == index_col).astype(BF16)


LANES = 128


def fill_rows(index_ref, hot_ref):
    for j in range(index_ref.shape[0]):
        hot_ref[:, j * LANES : (j + 1) * LANES] = onehot_rows(index_ref[j : j + 1, :], hot_ref.shape[0])


def fill_cols(index_ref, hot_ref):
    turned = jnp.transpose(index_ref[...])
    for j in range(index_ref.shape[0]):
        hot_ref[j * LANES : (j + 1) * LANES, :] = onehot_cols(turned[:, j : j + 1], hot_ref.shape[1])


def swish_parts(pre):
    sig = 0.5 * jnp.tanh(0.5 * pre) + 0.5
    value = pre * sig
    return value, sig + value * (1.0 - sig)


def norm_parts(raw):
    width = raw.shape[1]
    centred = raw - jnp.sum(raw, axis=1, keepdims=True) * (1.0 / width)
    spread = jnp.sum(centred * centred, axis=1, keepdims=True) * (1.0 / width)
    scale = lax.rsqrt(spread + EPSILON)
    return centred * scale, scale


def norm_back(grad, unit, scale):
    width = grad.shape[1]
    first = jnp.sum(grad, axis=1, keepdims=True) * (1.0 / width)
    second = jnp.sum(grad * unit, axis=1, keepdims=True) * (1.0 / width)
    return (grad - first - unit * second) * scale


def parity(axis):
    return lax.axis_index(axis) % 2


def pick_kernel(send_ref, mesh_ref, *refs):
    outs, picked = refs[:4], refs[4]
    hot = onehot_rows(send_ref[...], mesh_ref.shape[0])
    picked[...] = mm_tn(hot, mesh_ref[...]).astype(BF16)
    margin = outs[0].shape[0]
    for pair, axis in enumerate(("sector", "band")):
        odd = parity(axis)
        for turn in range(2):
            group = 2 * pair + (1 - odd if turn == 0 else odd)
            outs[2 * pair + turn][...] = picked[pl.ds(pl.multiple_of(group * margin, margin), margin), :]


def pick(send_rows, mesh_lat):
    n, width = send_rows.shape[0], mesh_lat.shape[1]
    part = jax.ShapeDtypeStruct((n // 4, width), BF16)
    return pl.pallas_call(
        pick_kernel,
        out_shape=[part] * 4,
        in_specs=[VM, VM],
        out_specs=[VM] * 4,
        scratch_shapes=[pltpu.VMEM((n, width), BF16)],
        name="pick",
        cost_estimate=pl.CostEstimate(flops=2 * n * n * width, bytes_accessed=2 * n * width * 2, transcendentals=0),
    )(send_rows.reshape(1, n), mesh_lat)


TILE = 512
VMEM_LIMIT = 58 << 20


def gray(value):
    return value ^ (value >> 1)


def z_code(z):
    return z ^ (3 * (z >> 2))


def piece_order():
    pieces = []
    for block in range(16):
        code = (block >> 3) | ((block >> 2) & 1) << 1 | ((block >> 1) & 1) << 2
        z = next(i for i in range(8) if z_code(i) == code)
        pieces.append((block & 1) * 8 + z)
    return pieces


NODE_TILE = 512


def main_kernel(*refs):
    (src_hbm, dst_hbm, mesh_hbm, r0_hbm, r1_hbm, r2_hbm, r3_hbm, eg_hbm, ng_hbm), refs = refs[:9], refs[9:]
    (edge_hbm, grid_hbm, cot_hbm, w1_hbm, w2_hbm, n1_hbm, n2_hbm), refs = refs[:7], refs[7:]
    (out_hbm, gg_hbm, own_hbm, far_s_hbm, near_b_hbm, far_b_hbm, sa_hbm, sb_hbm, ka_hbm, kb_hbm), refs = refs[:10], refs[10:]
    (src, dst, parts, eg, ng, edge, grid, cot, w1, w2, n1, n2), refs = refs[:12], refs[12:]
    (out, gg, own_grad, far_s, near_b, far_b, send_a, send_b, keep_a, keep_b), refs = refs[:10], refs[10:]
    table, prod, prod_g, hot_s, hot_d, hot_st, hot_dt, slope, unit, scale, msg, gp, d_pre, gw, borrowed, sems, out_sems = refs

    width = w2.shape[0]
    edges, points, rows_table = edge.shape[0], grid.shape[0], table.shape[0]
    own, margin = mesh_hbm.shape[0], r0_hbm.shape[0]
    tiles = [slice(t * TILE, (t + 1) * TILE) for t in range(edges // TILE)]
    nodes = [slice(t * NODE_TILE, (t + 1) * NODE_TILE) for t in range(points // NODE_TILE)]
    received = [parts.at[pl.ds(i * margin, margin), :] for i in range(4)]
    pairs = (
        (dst_hbm, dst),
        (src_hbm, src),
        (grid_hbm, grid),
        (w1_hbm, w1),
        (edge_hbm, edge),
        (mesh_hbm, table.at[pl.ds(0, own), :]),
        (r0_hbm, received[0]),
        (r1_hbm, received[1]),
        (r2_hbm, received[2]),
        (r3_hbm, received[3]),
        (w2_hbm, w2),
        (eg_hbm, eg),
        (n1_hbm, n1),
        (ng_hbm, ng),
        (n2_hbm, n2),
        (cot_hbm, cot),
    )
    copies = [pltpu.make_async_copy(source, target, sems.at[i]) for i, (source, target) in enumerate(pairs)]
    for copy in copies:
        copy.start()

    results = (
        (out, out_hbm),
        (send_a, sa_hbm),
        (send_b, sb_hbm),
        (keep_a, ka_hbm),
        (keep_b, kb_hbm),
        (near_b, near_b_hbm),
        (far_s, far_s_hbm),
        (far_b, far_b_hbm),
        (own_grad, own_hbm),
        (gg, gg_hbm),
    )
    stores = [pltpu.make_async_copy(source, target, out_sems.at[i]) for i, (source, target) in enumerate(results)]

    copies[0].wait()
    fill_cols(dst, hot_d)
    fill_rows(dst, hot_dt)
    copies[1].wait()
    fill_cols(src, hot_s)
    fill_rows(src, hot_st)
    starts = []
    for pair, axis in enumerate(("sector", "band")):
        odd = parity(axis)
        for slot in (1 - odd, odd):
            starts.append(pl.multiple_of((2 * pair + slot) * margin, margin))
    copies[2].wait()
    copies[3].wait()
    w_edge, w_mesh, w_grid = (w1.at[pl.ds(i * width, width), :] for i in range(3))
    prod_g[...] = mm(grid[...], w_grid[...]).astype(BF16)
    for copy in copies[5:10]:
        copy.wait()
    for start, part in zip(starts, received):
        table[pl.ds(own + start, margin), :] = part[...]
    prod[...] = mm(table[...], w_mesh[...]).astype(BF16)
    copies[4].wait()
    copies[10].wait()
    copies[11].wait()
    edge_gain = eg[...]
    for copy in copies[12:]:
        copy.wait()
    for rows in tiles:
        pre = mm(edge[rows, :], w_edge[...]) + mm(hot_s[rows, :], prod[...]) + mm(hot_d[rows, :], prod_g[...])
        hidden, steep = swish_parts(pre)
        slope[rows, :] = steep
        normed, inv = norm_parts(mm(hidden.astype(BF16), w2[...]))
        unit[rows, :] = normed
        scale[rows, :] = inv
        msg[rows, :] = (normed * edge_gain).astype(BF16)
    node_gain = ng[...]
    n1_agg, n1_grid = (n1.at[pl.ds(i * width, width), :] for i in range(2))
    d_agg = []
    for rows in nodes:
        agg = mm(hot_dt[rows, :], msg[...]).astype(BF16)
        node_hidden, node_slope = swish_parts(mm(agg, n1_agg[...]) + mm(grid[rows, :], n1_grid[...]))
        node_unit, node_inv = norm_parts(mm(node_hidden.astype(BF16), n2[...]))
        out[rows, :] = (grid[rows, :].astype(F32) + node_unit * node_gain).astype(BF16)
        d_raw = norm_back(cot[rows, :].astype(F32) * node_gain, node_unit, node_inv)
        d_hidden = mm_nt(d_raw.astype(BF16), n2[...]).astype(BF16).astype(F32)
        d_pre[rows, :] = (d_hidden * node_slope).astype(BF16)
        d_agg.append(mm_nt(d_pre[rows, :], n1_agg[...]).astype(BF16))
    stores[0].start()
    d_agg = jnp.concatenate(d_agg, axis=0)
    for rows in tiles:
        d_msg = mm(hot_d[rows, :], d_agg)
        d_edge = norm_back(d_msg * edge_gain, unit[rows, :], scale[rows, :])
        d_hid = mm_nt(d_edge.astype(BF16), w2[...]).astype(BF16).astype(F32)
        gp[rows, :] = (d_hid * slope[rows, :]).astype(BF16)
    sm = mm(hot_st[...], gp[...]).astype(BF16)
    sg = mm(hot_dt[...], gp[...]).astype(BF16)
    gw[width : 2 * width, :] = mm_tn(table[...], sm).astype(BF16)
    grad_table = mm_nt(sm, w_mesh[...])
    gw[2 * width : 3 * width, :] = mm_tn(grid[...], sg).astype(BF16)
    gw[0:width, :] = mm_tn(edge[...], gp[...]).astype(BF16)
    core = parity("sector")
    half, quarter = width // 2, width // 4
    own_grad[...] = grad_table[0:own]
    borrowed[...] = grad_table[own:].astype(BF16)
    near_s_rows, far_s_rows, near_b_rows, far_b_rows = (borrowed[pl.ds(start, margin), :] for start in starts)
    kept = keep_a.shape[0]
    for i in range(2):
        send_a[kept + i * margin : kept + (i + 1) * margin, :] = near_s_rows[:, i * half : (i + 1) * half]
    for i in range(4):
        near_b[i * margin : (i + 1) * margin, :] = near_b_rows[:, i * quarter : (i + 1) * quarter]
    far_s[...] = far_s_rows
    far_b[...] = far_b_rows
    piece = gw.shape[0] // (2 * len(piece_order()))
    for i, j in enumerate(piece_order()):
        rows = slice(i * piece, (i + 1) * piece)
        mine = pl.ds(pl.multiple_of((2 * j + core) * piece, piece), piece)
        other = pl.ds(pl.multiple_of((2 * j + 1 - core) * piece, piece), piece)
        send_a[rows, :] = gw[other, 0:half]
        send_b[rows, :] = gw[other, half:width]
        keep_a[rows, :] = gw[mine, 0:half]
        keep_b[rows, :] = gw[mine, half:width]
    for store in stores[1:9]:
        store.start()
    gg[...] = (cot[...].astype(F32) + mm_nt(d_pre[...], n1_grid[...]) + mm_nt(sg, w_grid[...])).astype(BF16)
    stores[9].start()
    for store in stores:
        store.wait()


def main(edge_src, edge_dst, mesh_lat, received, edge_gain, node_gain, edge_feat, grid_block, cot_block, w1, w2, n1, n2):
    edges, width = edge_feat.shape
    points, own = grid_block.shape[0], mesh_lat.shape[0]
    margin = received[0].shape[0]
    table = own + 4 * margin
    half, quarter, kept = width // 2, width // 4, 3 * width // 2
    operands = (
        edge_src.reshape(edges // LANES, LANES),
        edge_dst.reshape(edges // LANES, LANES),
        mesh_lat,
        *received,
        edge_gain.reshape(1, width),
        node_gain.reshape(1, width),
        edge_feat,
        grid_block,
        cot_block,
        w1,
        w2,
        n1,
        n2,
    )
    outs = [
        ((points, width), BF16),
        ((points, width), BF16),
        ((own, width), F32),
        ((margin, width), BF16),
        ((4 * margin, quarter), BF16),
        ((margin, width), BF16),
        ((kept + 2 * margin, half), BF16),
        ((kept, half), BF16),
        ((kept, half), BF16),
        ((kept, half), BF16),
    ]
    local = [pltpu.VMEM(x.shape, x.dtype) for x in operands]
    scratch = [
        ((table, width), BF16),
        ((table, width), BF16),
        ((points, width), BF16),
        ((edges, table), BF16),
        ((edges, points), BF16),
        ((table, edges), BF16),
        ((points, edges), BF16),
        ((edges, width), F32),
        ((edges, width), F32),
        ((edges, 1), F32),
        ((edges, width), BF16),
        ((edges, width), BF16),
        ((points, width), BF16),
        ((3 * width, width), BF16),
        ((4 * margin, width), BF16),
    ]
    return pl.pallas_call(
        main_kernel,
        out_shape=[jax.ShapeDtypeStruct(*shape) for shape in outs],
        in_specs=[ANY] * len(operands),
        out_specs=[ANY] * len(outs),
        scratch_shapes=local[:2]
        + [pltpu.VMEM((4 * margin, width), BF16)]
        + local[7:]
        + [pltpu.VMEM(*shape) for shape in outs + scratch]
        + [pltpu.SemaphoreType.DMA((len(operands),)), pltpu.SemaphoreType.DMA((len(outs),))],
        compiler_params=pltpu.CompilerParams(vmem_limit_bytes=VMEM_LIMIT),
        name="main",
        cost_estimate=pl.CostEstimate(
            flops=24 * edges * width * width,
            bytes_accessed=12 * edges * width,
            transcendentals=edges * width,
        ),
    )(*operands)


def mesh_kernel(send_ref, own_ref, near_s_ref, far_s_ref, near_b_ref, far_b_ref, out_ref, back):
    margin = far_s_ref.shape[0]
    width = far_s_ref.shape[1]
    for pair, (near, far) in enumerate(((near_s_ref, far_s_ref), (near_b_ref, far_b_ref))):
        odd = parity("band" if pair else "sector")
        first = pl.ds(pl.multiple_of((2 * pair + 1 - odd) * margin, margin), margin)
        second = pl.ds(pl.multiple_of((2 * pair + odd) * margin, margin), margin)
        for i in range(width // near.shape[1]):
            back[first, i * near.shape[1] : (i + 1) * near.shape[1]] = near[i * margin : (i + 1) * margin, :]
        back[second, :] = far[...]
    hot = onehot_rows(send_ref[...], own_ref.shape[0])
    out_ref[...] = (own_ref[...] + mm(hot, back[...])).astype(BF16)


def mesh_grads(send_rows, own, returned):
    n, width = send_rows.shape[0], own.shape[1]

    def tail(array):
        rows = n // 4 * width // array.shape[1]
        return pl.BlockSpec((rows, array.shape[1]), lambda i: (array.shape[0] // rows - 1, 0))

    whole = lambda array: pl.BlockSpec(array.shape, lambda i: (0, 0))
    send_row = send_rows.reshape(1, n)
    return pl.pallas_call(
        mesh_kernel,
        out_shape=jax.ShapeDtypeStruct(own.shape, BF16),
        grid=(1,),
        in_specs=[whole(send_row), whole(own)] + [tail(array) for array in returned],
        out_specs=whole(own),
        scratch_shapes=[pltpu.VMEM((n, width), BF16)],
        name="mesh_grads",
        cost_estimate=pl.CostEstimate(flops=2 * n * n * width, bytes_accessed=1 << 19, transcendentals=0),
    )(send_row, own, *returned)


def trade(part, axis, turn):
    devices = lax.axis_size(axis)
    last = devices if axis == "sector" else devices - 1
    ups = [(i, (i + 1) % devices) for i in range(turn, last, 2)]
    return lax.ppermute(part, axis, ups + [(j, i) for i, j in ups])


def swap(parts):
    return [trade(parts[2 * pair + turn], axis, turn) for pair, axis in enumerate(("sector", "band")) for turn in range(2)]


def coordinates(band, sector):
    return {
        "x_lo": band // 4,
        "y": gray(band % 4),
        "x_hi": sector // 16,
        "z": z_code(sector % 16 // 2),
        "core": sector % 2,
    }


def send(values, flips):
    place = {}
    for band in range(lax.axis_size("band")):
        for sector in range(lax.axis_size("sector")):
            place[tuple(coordinates(band, sector).values())] = band * lax.axis_size("sector") + sector
    names = list(coordinates(0, 0))
    pairs = []
    for spot, source in place.items():
        target = list(spot)
        for name, bit in flips:
            target[names.index(name)] ^= 1 << bit
        pairs.append((source, place[tuple(target)]))
    return lax.ppermute(values, ("band", "sector"), sorted(pairs))


def total(*terms):
    return sum(term.astype(F32) for term in terms).astype(BF16)


def plus(a, b):
    return total(a, b)


def reduce_weights(near_b, send_a, send_b, keep_a, keep_b, tails):
    here = coordinates(lax.axis_index("band"), lax.axis_index("sector"))

    def bit(name, k=0):
        return ((here[name] >> k) & 1) == 1

    def halve(low, high, name, k=0):
        mine = bit(name, k)
        return jnp.where(mine, high, low), send(jnp.where(mine, low, high), [(name, k)])

    def quarter(values, first, second):
        parts = values.reshape(2, 2, values.shape[0] // 4, values.shape[1])
        one, two = bit(*first), bit(*second)

        def part(swap_one, swap_two):
            low, high = (jnp.where(two != swap_two, row[1], row[0]) for row in parts)
            return jnp.where(one != swap_one, high, low)

        return part(False, False), send(part(True, False), [first]), send(part(False, True), [second]), send(part(True, True), [first, second])

    def halves(values, axis):
        return jnp.split(values, 2, axis=axis)

    near_s = got_a = send(send_a, [("core", 0)])
    part_a = plus(keep_a, got_a[: keep_a.shape[0]])
    part_b = plus(keep_b, send(send_b, [("core", 0)]))
    a, got_a = halve(*halves(part_a, 0), "z")
    left, right = halves(part_b, 1)
    mine = bit("y")
    b = jnp.where(mine, right, left)
    near_b = got_b = send(jnp.concatenate([jnp.where(mine, left, right), near_b], axis=0), [("y", 0)])
    got_b = got_b[: b.shape[0]]
    got_a, got_b = tails[0](part_b, got_a, got_b, near_s, near_b)
    a, got_a = halve(*halves(plus(a, got_a), 1), "y")
    b, got_b = halve(*halves(plus(b, got_b), 0), "z")
    got_a, got_b = tails[1](got_a, got_b)
    both = jnp.stack([plus(a, got_a).reshape(2, -1, a.shape[1]), plus(b, got_b).reshape(2, -1, a.shape[1])])
    held, *got = quarter(both.reshape(-1, a.shape[1]), ("x_lo", 0), ("z", 1))
    got = tails[2](*got)
    part = total(held, *got)
    held, *got = quarter(part, ("z", 2), ("x_hi", 0))
    got = tails[3](*got)
    part = total(held, *got)
    part = plus(part, send(part, [("y", 1)]))
    by_y = send(part, [("y", 0)])
    by_x = send(part, [("x_lo", 0)])
    by_both = send(part, [("y", 0), ("x_lo", 0)])
    odd_y, odd_x = bit("y"), bit("x_lo")

    def ordered(mine, other):
        return jnp.concatenate([jnp.where(odd_y, other, mine), jnp.where(odd_y, mine, other)], axis=1)

    near, far = ordered(part, by_y), ordered(by_x, by_both)
    return jnp.concatenate([jnp.where(odd_x, far, near), jnp.where(odd_x, near, far)], axis=1).astype(F32)


def shards(
    grid_lat,
    mesh_lat,
    edge_feat,
    edge_src,
    edge_dst,
    send_rows,
    w_edge1,
    w_edge2,
    edge_gain,
    w_node1,
    w_node2,
    node_gain,
    cotangent,
):
    lat_rows, lon_cols, width = grid_lat.shape
    grid_block = grid_lat.reshape(lat_rows * lon_cols, width)
    cot_block = cotangent.reshape(lat_rows * lon_cols, width)
    received = swap(pick(send_rows, mesh_lat))
    result, grad_grid, own_grad, far_s, near_b, far_b, *sums = main(
        edge_src, edge_dst, mesh_lat, received, edge_gain, node_gain, edge_feat, grid_block, cot_block, w_edge1, w_edge2, w_node1, w_node2
    )
    done = {}

    def after_first(part, got_a, got_b, near_s, near_b):
        far, _ = lax.optimization_barrier((far_s, part))
        done["far_s"] = trade(far, "sector", 1)
        done["near"] = near_s, near_b
        done["first"] = got_a
        return got_a, got_b

    def after_second(*got):
        far, _ = lax.optimization_barrier((far_b, done["first"]))
        done["far_b"] = trade(far, "band", 1)
        done["far_s"], *got = lax.optimization_barrier((done["far_s"], *got))
        return got

    def after_third(*got):
        done["far_b"], *got = lax.optimization_barrier((done["far_b"], *got))
        return got

    def after_fourth(*got):
        near_s, near_b = done["near"]
        grads = mesh_grads(send_rows, own_grad, (near_s, done["far_s"], near_b, done["far_b"]))
        done["mesh"], *got = lax.optimization_barrier((grads, *got))
        return got

    grad_w = reduce_weights(near_b, *sums, (after_first, after_second, after_third, after_fourth))
    total_edges = edge_feat.shape[0] * lax.axis_size("band") * lax.axis_size("sector")
    grad_w = grad_w * (1.0 / math.sqrt(total_edges))
    return (
        result.reshape(lat_rows, lon_cols, width),
        grad_grid.reshape(lat_rows, lon_cols, width),
        done["mesh"],
        grad_w,
    )


def solution(mesh):
    rows = P(("band", "sector"), None)
    flat = P(("band", "sector"))
    grid = P("band", "sector", None)
    in_specs = (grid, rows, rows, flat, flat, flat, P(), P(), P(), P(), P(), P(), grid)
    out_specs = (grid, grid, rows, P("sector", None))
    return jax.shard_map(shards, mesh=mesh, in_specs=in_specs, out_specs=out_specs, check_vma=False)
```

```python
import math

import jax
import jax.numpy as jnp
from jax import lax
from jax.experimental import pallas as pl
from jax.experimental.pallas import tpu as pltpu
from jax.sharding import PartitionSpec as P

EPSILON = 1e-05
BF16 = jnp.bfloat16
F32 = jnp.float32
HBM = pl.BlockSpec(memory_space=pltpu.HBM)
ANY = pl.BlockSpec(memory_space=pl.ANY)
VM = pl.BlockSpec(memory_space=pltpu.VMEM)


def mm(a, b):
    return lax.dot_general(a, b, (((1,), (0,)), ((), ())), preferred_element_type=F32)


def mm_nt(a, b):
    return lax.dot_general(a, b, (((1,), (1,)), ((), ())), preferred_element_type=F32)


def mm_tn(a, b):
    return lax.dot_general(a, b, (((0,), (0,)), ((), ())), preferred_element_type=F32)


def onehot_rows(index_row, rows):
    n = index_row.shape[1]
    return (lax.broadcasted_iota(jnp.int32, (rows, n), 0) == index_row).astype(BF16)


def onehot_cols(index_col, cols):
    n = index_col.shape[0]
    return (lax.broadcasted_iota(jnp.int32, (n, cols), 1) == index_col).astype(BF16)


LANES = 128


def fill_rows(index_ref, hot_ref):
    for j in range(index_ref.shape[0]):
        hot_ref[:, j * LANES : (j + 1) * LANES] = onehot_rows(index_ref[j : j + 1, :], hot_ref.shape[0])


def fill_cols(index_ref, hot_ref):
    turned = jnp.transpose(index_ref[...])
    for j in range(index_ref.shape[0]):
        hot_ref[j * LANES : (j + 1) * LANES, :] = onehot_cols(turned[:, j : j + 1], hot_ref.shape[1])


def swish_parts(pre):
    sig = 0.5 * jnp.tanh(0.5 * pre) + 0.5
    value = pre * sig
    return value, sig + value * (1.0 - sig)


def norm_parts(raw):
    width = raw.shape[1]
    centred = raw - jnp.sum(raw, axis=1, keepdims=True) * (1.0 / width)
    spread = jnp.sum(centred * centred, axis=1, keepdims=True) * (1.0 / width)
    scale = lax.rsqrt(spread + EPSILON)
    return centred * scale, scale


def norm_back(grad, unit, scale):
    width = grad.shape[1]
    first = jnp.sum(grad, axis=1, keepdims=True) * (1.0 / width)
    second = jnp.sum(grad * unit, axis=1, keepdims=True) * (1.0 / width)
    return (grad - first - unit * second) * scale


def parity(axis):
    return lax.axis_index(axis) % 2


def pick_kernel(send_ref, mesh_ref, *refs):
    outs, picked = refs[:4], refs[4]
    hot = onehot_rows(send_ref[...], mesh_ref.shape[0])
    picked[...] = mm_tn(hot, mesh_ref[...]).astype(BF16)
    margin = outs[0].shape[0]
    for pair, axis in enumerate(("sector", "band")):
        odd = parity(axis)
        for turn in range(2):
            group = 2 * pair + (1 - odd if turn == 0 else odd)
            outs[2 * pair + turn][...] = picked[pl.ds(pl.multiple_of(group * margin, margin), margin), :]


def pick(send_rows, mesh_lat):
    n, width = send_rows.shape[0], mesh_lat.shape[1]
    part = jax.ShapeDtypeStruct((n // 4, width), BF16)
    return pl.pallas_call(
        pick_kernel,
        out_shape=[part] * 4,
        in_specs=[VM, VM],
        out_specs=[VM] * 4,
        scratch_shapes=[pltpu.VMEM((n, width), BF16)],
        compiler_params=pltpu.CompilerParams(vmem_limit_bytes=8 << 20),
        name="pick",
        cost_estimate=pl.CostEstimate(flops=2 * n * n * width, bytes_accessed=2 * n * width * 2, transcendentals=0),
    )(*(pltpu.with_memory_space_constraint(x, pltpu.HBM) for x in (send_rows.reshape(1, n), mesh_lat)))


TILE = 512
VMEM_LIMIT = 44 << 20


def gray(value):
    return value ^ (value >> 1)


def z_code(z):
    return z ^ (3 * (z >> 2))


def piece_order():
    pieces = []
    for block in range(16):
        code = (block >> 3) | ((block >> 2) & 1) << 1 | ((block >> 1) & 1) << 2
        z = next(i for i in range(8) if z_code(i) == code)
        pieces.append((block & 1) * 8 + z)
    return pieces


NODE_TILE = 512


def main_kernel(*refs):
    (src_hbm, dst_hbm, mesh_hbm, r0_hbm, r1_hbm, r2_hbm, r3_hbm, eg_hbm, ng_hbm), refs = refs[:9], refs[9:]
    (edge_hbm, grid_hbm, cot_hbm, w1_hbm, w2_hbm, n1_hbm, n2_hbm), refs = refs[:7], refs[7:]
    (out_hbm, gg_hbm, own_hbm, far_s_hbm, near_b_hbm, far_b_hbm, sa_hbm, sb_hbm, ka_hbm, kb_hbm), refs = refs[:10], refs[10:]
    (src, dst, parts, eg, ng, edge, grid, cot, w1, w2, n1, n2), refs = refs[:12], refs[12:]
    (out, gg, own_grad, far_s, near_b, far_b, send_a, send_b, keep_a, keep_b), refs = refs[:10], refs[10:]
    table, prod, prod_g, hot_s, hot_d, hot_st, hot_dt, slope, unit, scale, msg, gp, d_pre, gw, borrowed, sems, out_sems = refs

    width = w2.shape[0]
    edges, points, rows_table = edge.shape[0], grid.shape[0], table.shape[0]
    own, margin = mesh_hbm.shape[0], r0_hbm.shape[0]
    tiles = [slice(t * TILE, (t + 1) * TILE) for t in range(edges // TILE)]
    nodes = [slice(t * NODE_TILE, (t + 1) * NODE_TILE) for t in range(points // NODE_TILE)]
    received = [parts.at[pl.ds(i * margin, margin), :] for i in range(4)]
    pairs = (
        (dst_hbm, dst),
        (src_hbm, src),
        (grid_hbm, grid),
        (w1_hbm, w1),
        (edge_hbm, edge),
        (mesh_hbm, table.at[pl.ds(0, own), :]),
        (r0_hbm, received[0]),
        (r1_hbm, received[1]),
        (r2_hbm, received[2]),
        (r3_hbm, received[3]),
        (w2_hbm, w2),
        (eg_hbm, eg),
        (n1_hbm, n1),
        (ng_hbm, ng),
        (n2_hbm, n2),
        (cot_hbm, cot),
    )
    copies = [pltpu.make_async_copy(source, target, sems.at[i]) for i, (source, target) in enumerate(pairs)]
    for copy in copies:
        copy.start()

    results = (
        (out, out_hbm),
        (send_a, sa_hbm),
        (send_b, sb_hbm),
        (keep_a, ka_hbm),
        (keep_b, kb_hbm),
        (near_b, near_b_hbm),
        (far_s, far_s_hbm),
        (far_b, far_b_hbm),
        (own_grad, own_hbm),
        (gg, gg_hbm),
    )
    stores = [pltpu.make_async_copy(source, target, out_sems.at[i]) for i, (source, target) in enumerate(results)]

    copies[0].wait()
    fill_cols(dst, hot_d)
    fill_rows(dst, hot_dt)
    copies[1].wait()
    fill_cols(src, hot_s)
    fill_rows(src, hot_st)
    starts = []
    for pair, axis in enumerate(("sector", "band")):
        odd = parity(axis)
        for slot in (1 - odd, odd):
            starts.append(pl.multiple_of((2 * pair + slot) * margin, margin))
    copies[2].wait()
    copies[3].wait()
    w_edge, w_mesh, w_grid = (w1.at[pl.ds(i * width, width), :] for i in range(3))
    prod_g[...] = mm(grid[...], w_grid[...]).astype(BF16)
    for copy in copies[5:10]:
        copy.wait()
    for start, part in zip(starts, received):
        table[pl.ds(own + start, margin), :] = part[...]
    prod[...] = mm(table[...], w_mesh[...]).astype(BF16)
    copies[4].wait()
    copies[10].wait()
    copies[11].wait()
    edge_gain = eg[...]
    for copy in copies[12:]:
        copy.wait()
    for rows in tiles:
        pre = mm(edge[rows, :], w_edge[...]) + mm(hot_s[rows, :], prod[...]) + mm(hot_d[rows, :], prod_g[...])
        hidden, steep = swish_parts(pre)
        slope[rows, :] = steep
        normed, inv = norm_parts(mm(hidden.astype(BF16), w2[...]))
        unit[rows, :] = normed
        scale[rows, :] = inv
        msg[rows, :] = (normed * edge_gain).astype(BF16)
    node_gain = ng[...]
    n1_agg, n1_grid = (n1.at[pl.ds(i * width, width), :] for i in range(2))
    d_agg = []
    for rows in nodes:
        agg = mm(hot_dt[rows, :], msg[...]).astype(BF16)
        node_hidden, node_slope = swish_parts(mm(agg, n1_agg[...]) + mm(grid[rows, :], n1_grid[...]))
        node_unit, node_inv = norm_parts(mm(node_hidden.astype(BF16), n2[...]))
        out[rows, :] = (grid[rows, :].astype(F32) + node_unit * node_gain).astype(BF16)
        d_raw = norm_back(cot[rows, :].astype(F32) * node_gain, node_unit, node_inv)
        d_hidden = mm_nt(d_raw.astype(BF16), n2[...]).astype(BF16).astype(F32)
        d_pre[rows, :] = (d_hidden * node_slope).astype(BF16)
        d_agg.append(mm_nt(d_pre[rows, :], n1_agg[...]).astype(BF16))
    stores[0].start()
    d_agg = jnp.concatenate(d_agg, axis=0)
    for rows in tiles:
        d_msg = mm(hot_d[rows, :], d_agg)
        d_edge = norm_back(d_msg * edge_gain, unit[rows, :], scale[rows, :])
        d_hid = mm_nt(d_edge.astype(BF16), w2[...]).astype(BF16).astype(F32)
        gp[rows, :] = (d_hid * slope[rows, :]).astype(BF16)
    sm = mm(hot_st[...], gp[...]).astype(BF16)
    sg = mm(hot_dt[...], gp[...]).astype(BF16)
    gw[width : 2 * width, :] = mm_tn(table[...], sm).astype(BF16)
    grad_table = mm_nt(sm, w_mesh[...])
    gw[2 * width : 3 * width, :] = mm_tn(grid[...], sg).astype(BF16)
    gw[0:width, :] = mm_tn(edge[...], gp[...]).astype(BF16)
    core = parity("sector")
    half, quarter = width // 2, width // 4
    own_grad[...] = grad_table[0:own]
    borrowed[...] = grad_table[own:].astype(BF16)
    near_s_rows, far_s_rows, near_b_rows, far_b_rows = (borrowed[pl.ds(start, margin), :] for start in starts)
    kept = keep_a.shape[0]
    for i in range(2):
        send_a[kept + i * margin : kept + (i + 1) * margin, :] = near_s_rows[:, i * half : (i + 1) * half]
    for i in range(4):
        near_b[i * margin : (i + 1) * margin, :] = near_b_rows[:, i * quarter : (i + 1) * quarter]
    far_s[...] = far_s_rows
    far_b[...] = far_b_rows
    piece = gw.shape[0] // (2 * len(piece_order()))
    for i, j in enumerate(piece_order()):
        rows = slice(i * piece, (i + 1) * piece)
        mine = pl.ds(pl.multiple_of((2 * j + core) * piece, piece), piece)
        other = pl.ds(pl.multiple_of((2 * j + 1 - core) * piece, piece), piece)
        send_a[rows, :] = gw[other, 0:half]
        send_b[rows, :] = gw[other, half:width]
        keep_a[rows, :] = gw[mine, 0:half]
        keep_b[rows, :] = gw[mine, half:width]
    for store in stores[1:9]:
        store.start()
    gg[...] = (cot[...].astype(F32) + mm_nt(d_pre[...], n1_grid[...]) + mm_nt(sg, w_grid[...])).astype(BF16)
    stores[9].start()
    for store in stores:
        store.wait()


def main(edge_src, edge_dst, mesh_lat, received, edge_gain, node_gain, edge_feat, grid_block, cot_block, w1, w2, n1, n2):
    edges, width = edge_feat.shape
    points, own = grid_block.shape[0], mesh_lat.shape[0]
    margin = received[0].shape[0]
    table = own + 4 * margin
    half, quarter, kept = width // 2, width // 4, 3 * width // 2
    operands = (
        edge_src.reshape(edges // LANES, LANES),
        edge_dst.reshape(edges // LANES, LANES),
        mesh_lat,
        *received,
        edge_gain.reshape(1, width),
        node_gain.reshape(1, width),
        edge_feat,
        grid_block,
        cot_block,
        w1,
        w2,
        n1,
        n2,
    )
    outs = [
        ((points, width), BF16),
        ((points, width), BF16),
        ((own, width), F32),
        ((margin, width), BF16),
        ((4 * margin, quarter), BF16),
        ((margin, width), BF16),
        ((kept + 2 * margin, half), BF16),
        ((kept, half), BF16),
        ((kept, half), BF16),
        ((kept, half), BF16),
    ]
    local = [pltpu.VMEM(x.shape, x.dtype) for x in operands]
    scratch = [
        ((table, width), BF16),
        ((table, width), BF16),
        ((points, width), BF16),
        ((edges, table), BF16),
        ((edges, points), BF16),
        ((table, edges), BF16),
        ((points, edges), BF16),
        ((edges, width), F32),
        ((edges, width), F32),
        ((edges, 1), F32),
        ((edges, width), BF16),
        ((edges, width), BF16),
        ((points, width), BF16),
        ((3 * width, width), BF16),
        ((4 * margin, width), BF16),
    ]
    return pl.pallas_call(
        main_kernel,
        out_shape=[jax.ShapeDtypeStruct(*shape) for shape in outs],
        in_specs=[HBM] * 3 + [ANY] * 4 + [HBM] * (len(operands) - 7),
        out_specs=[HBM] * 3 + [ANY] * (len(outs) - 3),
        scratch_shapes=local[:2]
        + [pltpu.VMEM((4 * margin, width), BF16)]
        + local[7:]
        + [pltpu.VMEM(*shape) for shape in outs + scratch]
        + [pltpu.SemaphoreType.DMA((len(operands),)), pltpu.SemaphoreType.DMA((len(outs),))],
        compiler_params=pltpu.CompilerParams(vmem_limit_bytes=VMEM_LIMIT),
        name="main",
        cost_estimate=pl.CostEstimate(
            flops=24 * edges * width * width,
            bytes_accessed=12 * edges * width,
            transcendentals=edges * width,
        ),
    )(*[x if 3 <= i < 7 else pltpu.with_memory_space_constraint(x, pltpu.HBM) for i, x in enumerate(operands)])


def mesh_kernel(send_ref, own_ref, near_s_ref, far_s_ref, near_b_ref, far_b_ref, out_ref, back):
    margin = far_s_ref.shape[0]
    width = far_s_ref.shape[1]
    for pair, (near, far) in enumerate(((near_s_ref, far_s_ref), (near_b_ref, far_b_ref))):
        odd = parity("band" if pair else "sector")
        first = pl.ds(pl.multiple_of((2 * pair + 1 - odd) * margin, margin), margin)
        second = pl.ds(pl.multiple_of((2 * pair + odd) * margin, margin), margin)
        for i in range(width // near.shape[1]):
            back[first, i * near.shape[1] : (i + 1) * near.shape[1]] = near[i * margin : (i + 1) * margin, :]
        back[second, :] = far[...]
    hot = onehot_rows(send_ref[...], own_ref.shape[0])
    out_ref[...] = (own_ref[...] + mm(hot, back[...])).astype(BF16)


def mesh_grads(send_rows, own, returned):
    n, width = send_rows.shape[0], own.shape[1]

    def tail(array):
        rows = n // 4 * width // array.shape[1]
        return pl.BlockSpec((rows, array.shape[1]), lambda i: (array.shape[0] // rows - 1, 0))

    whole = lambda array: pl.BlockSpec(array.shape, lambda i: (0, 0))
    send_row = send_rows.reshape(1, n)
    return pl.pallas_call(
        mesh_kernel,
        out_shape=jax.ShapeDtypeStruct(own.shape, BF16),
        grid=(1,),
        in_specs=[whole(send_row), whole(own)] + [tail(array) for array in returned],
        out_specs=whole(own),
        scratch_shapes=[pltpu.VMEM((n, width), BF16)],
        compiler_params=pltpu.CompilerParams(vmem_limit_bytes=8 << 20),
        name="mesh_grads",
        cost_estimate=pl.CostEstimate(flops=2 * n * n * width, bytes_accessed=1 << 19, transcendentals=0),
    )(send_row, own, *returned)


def trade(part, axis, turn):
    devices = lax.axis_size(axis)
    last = devices if axis == "sector" else devices - 1
    ups = [(i, (i + 1) % devices) for i in range(turn, last, 2)]
    return lax.ppermute(part, axis, ups + [(j, i) for i, j in ups])


def swap(parts):
    return [trade(parts[2 * pair + turn], axis, turn) for pair, axis in enumerate(("sector", "band")) for turn in range(2)]


def coordinates(band, sector):
    return {
        "x_lo": band // 4,
        "y": gray(band % 4),
        "x_hi": sector // 16,
        "z": z_code(sector % 16 // 2),
        "core": sector % 2,
    }


def send(values, flips):
    place = {}
    for band in range(lax.axis_size("band")):
        for sector in range(lax.axis_size("sector")):
            place[tuple(coordinates(band, sector).values())] = band * lax.axis_size("sector") + sector
    names = list(coordinates(0, 0))
    pairs = []
    for spot, source in place.items():
        target = list(spot)
        for name, bit in flips:
            target[names.index(name)] ^= 1 << bit
        pairs.append((source, place[tuple(target)]))
    return lax.ppermute(values, ("band", "sector"), sorted(pairs))


def total(*terms):
    return sum(term.astype(F32) for term in terms).astype(BF16)


def plus(a, b):
    return total(a, b)


def reduce_weights(near_b, send_a, send_b, keep_a, keep_b, tails):
    here = coordinates(lax.axis_index("band"), lax.axis_index("sector"))

    def bit(name, k=0):
        return ((here[name] >> k) & 1) == 1

    def halve(low, high, name, k=0):
        mine = bit(name, k)
        return jnp.where(mine, high, low), send(jnp.where(mine, low, high), [(name, k)])

    def quarter(values, first, second):
        parts = values.reshape(2, 2, values.shape[0] // 4, values.shape[1])
        one, two = bit(*first), bit(*second)

        def part(swap_one, swap_two):
            low, high = (jnp.where(two != swap_two, row[1], row[0]) for row in parts)
            return jnp.where(one != swap_one, high, low)

        return part(False, False), send(part(True, False), [first]), send(part(False, True), [second]), send(part(True, True), [first, second])

    def halves(values, axis):
        return jnp.split(values, 2, axis=axis)

    near_s = got_a = send(send_a, [("core", 0)])
    part_a = plus(keep_a, got_a[: keep_a.shape[0]])
    part_b = plus(keep_b, send(send_b, [("core", 0)]))
    a, got_a = halve(*halves(part_a, 0), "z")
    left, right = halves(part_b, 1)
    mine = bit("y")
    b = jnp.where(mine, right, left)
    near_b = got_b = send(jnp.concatenate([jnp.where(mine, left, right), near_b], axis=0), [("y", 0)])
    got_b = got_b[: b.shape[0]]
    got_a, got_b = tails[0](part_b, got_a, got_b, near_s, near_b)
    a, got_a = halve(*halves(plus(a, got_a), 1), "y")
    b, got_b = halve(*halves(plus(b, got_b), 0), "z")
    got_a, got_b = tails[1](got_a, got_b)
    both = jnp.stack([plus(a, got_a).reshape(2, -1, a.shape[1]), plus(b, got_b).reshape(2, -1, a.shape[1])])
    held, *got = quarter(both.reshape(-1, a.shape[1]), ("x_lo", 0), ("z", 1))
    part = total(held, *got)
    held, *got = quarter(part, ("z", 2), ("x_hi", 0))
    part = total(held, *got)
    part = plus(part, send(part, [("y", 1)]))
    by_y = send(part, [("y", 0)])
    by_x = send(part, [("x_lo", 0)])
    by_both = send(part, [("y", 0), ("x_lo", 0)])
    odd_y, odd_x = bit("y"), bit("x_lo")

    def ordered(mine, other):
        return jnp.concatenate([jnp.where(odd_y, other, mine), jnp.where(odd_y, mine, other)], axis=1)

    near, far = ordered(part, by_y), ordered(by_x, by_both)
    return jnp.concatenate([jnp.where(odd_x, far, near), jnp.where(odd_x, near, far)], axis=1).astype(F32)


def shards(
    grid_lat,
    mesh_lat,
    edge_feat,
    edge_src,
    edge_dst,
    send_rows,
    w_edge1,
    w_edge2,
    edge_gain,
    w_node1,
    w_node2,
    node_gain,
    cotangent,
):
    lat_rows, lon_cols, width = grid_lat.shape
    grid_block = grid_lat.reshape(lat_rows * lon_cols, width)
    cot_block = cotangent.reshape(lat_rows * lon_cols, width)
    received = swap(pick(send_rows, mesh_lat))
    result, grad_grid, own_grad, far_s, near_b, far_b, *sums = main(
        edge_src, edge_dst, mesh_lat, received, edge_gain, node_gain, edge_feat, grid_block, cot_block, w_edge1, w_edge2, w_node1, w_node2
    )
    done = {}

    def after_first(part, got_a, got_b, near_s, near_b):
        far, other, _ = lax.optimization_barrier((far_s, far_b, part))
        far, other, *got = lax.optimization_barrier((trade(far, "sector", 1), trade(other, "band", 1), got_a, got_b))
        done["back"] = near_s, far, near_b, other
        return got

    def after_second(*got):
        done["mesh"], *got = lax.optimization_barrier((mesh_grads(send_rows, own_grad, done["back"]), *got))
        return got

    grad_w = reduce_weights(near_b, *sums, (after_first, after_second))
    total_edges = edge_feat.shape[0] * lax.axis_size("band") * lax.axis_size("sector")
    grad_w = grad_w * (1.0 / math.sqrt(total_edges))
    return (
        result.reshape(lat_rows, lon_cols, width),
        grad_grid.reshape(lat_rows, lon_cols, width),
        done["mesh"],
        grad_w,
    )


def solution(mesh):
    rows = P(("band", "sector"), None)
    flat = P(("band", "sector"))
    grid = P("band", "sector", None)
    in_specs = (grid, rows, rows, flat, flat, flat, P(), P(), P(), P(), P(), P(), grid)
    out_specs = (grid, grid, rows, P("sector", None))
    return jax.shard_map(shards, mesh=mesh, in_specs=in_specs, out_specs=out_specs, check_vma=False)
```

```python
import math

import jax
import jax.numpy as jnp
from jax import lax
from jax.experimental import pallas as pl
from jax.experimental.pallas import tpu as pltpu
from jax.sharding import PartitionSpec as P

EPSILON = 1e-05
BF16 = jnp.bfloat16
F32 = jnp.float32
HBM = pl.BlockSpec(memory_space=pltpu.HBM)
ANY = pl.BlockSpec(memory_space=pl.ANY)
VM = pl.BlockSpec(memory_space=pltpu.VMEM)


def mm(a, b):
    return lax.dot_general(a, b, (((1,), (0,)), ((), ())), preferred_element_type=F32)


def mm_nt(a, b):
    return lax.dot_general(a, b, (((1,), (1,)), ((), ())), preferred_element_type=F32)


def mm_tn(a, b):
    return lax.dot_general(a, b, (((0,), (0,)), ((), ())), preferred_element_type=F32)


def onehot_rows(index_row, rows):
    n = index_row.shape[1]
    return (lax.broadcasted_iota(jnp.int32, (rows, n), 0) == index_row).astype(BF16)


def onehot_cols(index_col, cols):
    n = index_col.shape[0]
    return (lax.broadcasted_iota(jnp.int32, (n, cols), 1) == index_col).astype(BF16)


LANES = 128


def fill_rows(index_ref, hot_ref):
    for j in range(index_ref.shape[0]):
        hot_ref[:, j * LANES : (j + 1) * LANES] = onehot_rows(index_ref[j : j + 1, :], hot_ref.shape[0])


def fill_cols(index_ref, hot_ref):
    turned = jnp.transpose(index_ref[...])
    for j in range(index_ref.shape[0]):
        hot_ref[j * LANES : (j + 1) * LANES, :] = onehot_cols(turned[:, j : j + 1], hot_ref.shape[1])


def swish_parts(pre):
    sig = 0.5 * jnp.tanh(0.5 * pre) + 0.5
    value = pre * sig
    return value, sig + value * (1.0 - sig)


def norm_parts(raw):
    width = raw.shape[1]
    centred = raw - jnp.sum(raw, axis=1, keepdims=True) * (1.0 / width)
    spread = jnp.sum(centred * centred, axis=1, keepdims=True) * (1.0 / width)
    scale = lax.rsqrt(spread + EPSILON)
    return centred * scale, scale


def norm_back(grad, unit, scale):
    width = grad.shape[1]
    first = jnp.sum(grad, axis=1, keepdims=True) * (1.0 / width)
    second = jnp.sum(grad * unit, axis=1, keepdims=True) * (1.0 / width)
    return (grad - first - unit * second) * scale


def parity(axis):
    return lax.axis_index(axis) % 2


def pick_kernel(send_ref, mesh_ref, *refs):
    outs, picked = refs[:4], refs[4]
    hot = onehot_rows(send_ref[...], mesh_ref.shape[0])
    picked[...] = mm_tn(hot, mesh_ref[...]).astype(BF16)
    margin = outs[0].shape[0]
    for pair, axis in enumerate(("sector", "band")):
        odd = parity(axis)
        for turn in range(2):
            group = 2 * pair + (1 - odd if turn == 0 else odd)
            outs[2 * pair + turn][...] = picked[pl.ds(pl.multiple_of(group * margin, margin), margin), :]


def pick(send_rows, mesh_lat):
    n, width = send_rows.shape[0], mesh_lat.shape[1]
    part = jax.ShapeDtypeStruct((n // 4, width), BF16)
    return pl.pallas_call(
        pick_kernel,
        out_shape=[part] * 4,
        in_specs=[VM, VM],
        out_specs=[VM] * 4,
        scratch_shapes=[pltpu.VMEM((n, width), BF16)],
        compiler_params=pltpu.CompilerParams(vmem_limit_bytes=8 << 20),
        name="pick",
        cost_estimate=pl.CostEstimate(flops=2 * n * n * width, bytes_accessed=2 * n * width * 2, transcendentals=0),
    )(*(pltpu.with_memory_space_constraint(x, pltpu.HBM) for x in (send_rows.reshape(1, n), mesh_lat)))


TILE = 512
VMEM_LIMIT = 44 << 20


def gray(value):
    return value ^ (value >> 1)


def z_code(z):
    return z ^ (3 * (z >> 2))


def piece_order():
    pieces = []
    for block in range(16):
        code = (block >> 3) | ((block >> 2) & 1) << 1 | ((block >> 1) & 1) << 2
        z = next(i for i in range(8) if z_code(i) == code)
        pieces.append((block & 1) * 8 + z)
    return pieces


NODE_TILE = 512


def main_kernel(*refs):
    (src_hbm, dst_hbm, mesh_hbm, r0_hbm, r1_hbm, r2_hbm, r3_hbm, eg_hbm, ng_hbm), refs = refs[:9], refs[9:]
    (edge_hbm, grid_hbm, cot_hbm, w1_hbm, w2_hbm, n1_hbm, n2_hbm), refs = refs[:7], refs[7:]
    (out_hbm, gg_hbm, own_hbm, far_s_hbm, near_b_hbm, far_b_hbm, sa_hbm, sb_hbm, ka_hbm, kb_hbm), refs = refs[:10], refs[10:]
    (src, dst, parts, eg, ng, edge, grid, cot, w1, w2, n1, n2), refs = refs[:12], refs[12:]
    (out, gg, own_grad, far_s, near_b, far_b, send_a, send_b, keep_a, keep_b), refs = refs[:10], refs[10:]
    table, prod, prod_g, hot_s, hot_d, hot_st, hot_dt, slope, unit, scale, msg, gp, d_pre, gw, borrowed, sems, out_sems = refs

    width = w2.shape[0]
    edges, points, rows_table = edge.shape[0], grid.shape[0], table.shape[0]
    own, margin = mesh_hbm.shape[0], r0_hbm.shape[0]
    tiles = [slice(t * TILE, (t + 1) * TILE) for t in range(edges // TILE)]
    nodes = [slice(t * NODE_TILE, (t + 1) * NODE_TILE) for t in range(points // NODE_TILE)]
    received = [parts.at[pl.ds(i * margin, margin), :] for i in range(4)]
    pairs = (
        (dst_hbm, dst),
        (src_hbm, src),
        (grid_hbm, grid),
        (w1_hbm, w1),
        (edge_hbm, edge),
        (mesh_hbm, table.at[pl.ds(0, own), :]),
        (r0_hbm, received[0]),
        (r1_hbm, received[1]),
        (r2_hbm, received[2]),
        (r3_hbm, received[3]),
        (w2_hbm, w2),
        (eg_hbm, eg),
        (n1_hbm, n1),
        (ng_hbm, ng),
        (n2_hbm, n2),
        (cot_hbm, cot),
    )
    copies = [pltpu.make_async_copy(source, target, sems.at[i]) for i, (source, target) in enumerate(pairs)]
    for copy in copies:
        copy.start()

    results = (
        (out, out_hbm),
        (send_a, sa_hbm),
        (send_b, sb_hbm),
        (keep_a, ka_hbm),
        (keep_b, kb_hbm),
        (near_b, near_b_hbm),
        (far_s, far_s_hbm),
        (far_b, far_b_hbm),
        (own_grad, own_hbm),
        (gg, gg_hbm),
    )
    stores = [pltpu.make_async_copy(source, target, out_sems.at[i]) for i, (source, target) in enumerate(results)]

    copies[0].wait()
    fill_cols(dst, hot_d)
    fill_rows(dst, hot_dt)
    copies[1].wait()
    fill_cols(src, hot_s)
    fill_rows(src, hot_st)
    starts = []
    for pair, axis in enumerate(("sector", "band")):
        odd = parity(axis)
        for slot in (1 - odd, odd):
            starts.append(pl.multiple_of((2 * pair + slot) * margin, margin))
    copies[2].wait()
    copies[3].wait()
    w_edge, w_mesh, w_grid = (w1.at[pl.ds(i * width, width), :] for i in range(3))
    prod_g[...] = mm(grid[...], w_grid[...]).astype(BF16)
    for copy in copies[5:10]:
        copy.wait()
    for start, part in zip(starts, received):
        table[pl.ds(own + start, margin), :] = part[...]
    prod[...] = mm(table[...], w_mesh[...]).astype(BF16)
    copies[4].wait()
    copies[10].wait()
    copies[11].wait()
    edge_gain = eg[...]
    for copy in copies[12:]:
        copy.wait()
    for rows in tiles:
        pre = mm(edge[rows, :], w_edge[...]) + mm(hot_s[rows, :], prod[...]) + mm(hot_d[rows, :], prod_g[...])
        hidden, steep = swish_parts(pre)
        slope[rows, :] = steep
        normed, inv = norm_parts(mm(hidden.astype(BF16), w2[...]))
        unit[rows, :] = normed
        scale[rows, :] = inv
        msg[rows, :] = (normed * edge_gain).astype(BF16)
    node_gain = ng[...]
    n1_agg, n1_grid = (n1.at[pl.ds(i * width, width), :] for i in range(2))
    d_agg = []
    for rows in nodes:
        agg = mm(hot_dt[rows, :], msg[...]).astype(BF16)
        node_hidden, node_slope = swish_parts(mm(agg, n1_agg[...]) + mm(grid[rows, :], n1_grid[...]))
        node_unit, node_inv = norm_parts(mm(node_hidden.astype(BF16), n2[...]))
        out[rows, :] = (grid[rows, :].astype(F32) + node_unit * node_gain).astype(BF16)
        d_raw = norm_back(cot[rows, :].astype(F32) * node_gain, node_unit, node_inv)
        d_hidden = mm_nt(d_raw.astype(BF16), n2[...]).astype(BF16).astype(F32)
        d_pre[rows, :] = (d_hidden * node_slope).astype(BF16)
        d_agg.append(mm_nt(d_pre[rows, :], n1_agg[...]).astype(BF16))
    d_agg = jnp.concatenate(d_agg, axis=0)
    for rows in tiles:
        d_msg = mm(hot_d[rows, :], d_agg)
        d_edge = norm_back(d_msg * edge_gain, unit[rows, :], scale[rows, :])
        d_hid = mm_nt(d_edge.astype(BF16), w2[...]).astype(BF16).astype(F32)
        gp[rows, :] = (d_hid * slope[rows, :]).astype(BF16)
    sm = mm(hot_st[...], gp[...]).astype(BF16)
    sg = mm(hot_dt[...], gp[...]).astype(BF16)
    grad_table = mm_nt(sm, w_mesh[...])
    gg[...] = (cot[...].astype(F32) + mm_nt(d_pre[...], n1_grid[...]) + mm_nt(sg, w_grid[...])).astype(BF16)
    core = parity("sector")
    half, quarter = width // 2, width // 4
    own_grad[...] = grad_table[0:own]
    borrowed[...] = grad_table[own:].astype(BF16)
    near_s_rows, far_s_rows, near_b_rows, far_b_rows = (borrowed[pl.ds(start, margin), :] for start in starts)
    kept = keep_a.shape[0]
    for i in range(2):
        send_a[kept + i * margin : kept + (i + 1) * margin, :] = near_s_rows[:, i * half : (i + 1) * half]
    for i in range(4):
        near_b[i * margin : (i + 1) * margin, :] = near_b_rows[:, i * quarter : (i + 1) * quarter]
    far_s[...] = far_s_rows
    far_b[...] = far_b_rows
    early = [stores[0], *stores[5:]]
    for store in early:
        store.start()
    gw[width : 2 * width, :] = mm_tn(table[...], sm).astype(BF16)
    gw[2 * width : 3 * width, :] = mm_tn(grid[...], sg).astype(BF16)
    gw[0:width, :] = mm_tn(edge[...], gp[...]).astype(BF16)
    piece = gw.shape[0] // (2 * len(piece_order()))
    for i, j in enumerate(piece_order()):
        rows = slice(i * piece, (i + 1) * piece)
        mine = pl.ds(pl.multiple_of((2 * j + core) * piece, piece), piece)
        other = pl.ds(pl.multiple_of((2 * j + 1 - core) * piece, piece), piece)
        send_a[rows, :] = gw[other, 0:half]
        send_b[rows, :] = gw[other, half:width]
        keep_a[rows, :] = gw[mine, 0:half]
        keep_b[rows, :] = gw[mine, half:width]
    for store in stores[1:5]:
        store.start()
    for store in stores:
        store.wait()


def main(edge_src, edge_dst, mesh_lat, received, edge_gain, node_gain, edge_feat, grid_block, cot_block, w1, w2, n1, n2):
    edges, width = edge_feat.shape
    points, own = grid_block.shape[0], mesh_lat.shape[0]
    margin = received[0].shape[0]
    table = own + 4 * margin
    half, quarter, kept = width // 2, width // 4, 3 * width // 2
    operands = (
        edge_src.reshape(edges // LANES, LANES),
        edge_dst.reshape(edges // LANES, LANES),
        mesh_lat,
        *received,
        edge_gain.reshape(1, width),
        node_gain.reshape(1, width),
        edge_feat,
        grid_block,
        cot_block,
        w1,
        w2,
        n1,
        n2,
    )
    outs = [
        ((points, width), BF16),
        ((points, width), BF16),
        ((own, width), F32),
        ((margin, width), BF16),
        ((4 * margin, quarter), BF16),
        ((margin, width), BF16),
        ((kept + 2 * margin, half), BF16),
        ((kept, half), BF16),
        ((kept, half), BF16),
        ((kept, half), BF16),
    ]
    local = [pltpu.VMEM(x.shape, x.dtype) for x in operands]
    scratch = [
        ((table, width), BF16),
        ((table, width), BF16),
        ((points, width), BF16),
        ((edges, table), BF16),
        ((edges, points), BF16),
        ((table, edges), BF16),
        ((points, edges), BF16),
        ((edges, width), F32),
        ((edges, width), F32),
        ((edges, 1), F32),
        ((edges, width), BF16),
        ((edges, width), BF16),
        ((points, width), BF16),
        ((3 * width, width), BF16),
        ((4 * margin, width), BF16),
    ]
    return pl.pallas_call(
        main_kernel,
        out_shape=[jax.ShapeDtypeStruct(*shape) for shape in outs],
        in_specs=[HBM] * 3 + [ANY] * 4 + [HBM] * (len(operands) - 7),
        out_specs=[HBM] * 3 + [ANY] * (len(outs) - 3),
        scratch_shapes=local[:2]
        + [pltpu.VMEM((4 * margin, width), BF16)]
        + local[7:]
        + [pltpu.VMEM(*shape) for shape in outs + scratch]
        + [pltpu.SemaphoreType.DMA((len(operands),)), pltpu.SemaphoreType.DMA((len(outs),))],
        compiler_params=pltpu.CompilerParams(vmem_limit_bytes=VMEM_LIMIT),
        name="main",
        cost_estimate=pl.CostEstimate(
            flops=24 * edges * width * width,
            bytes_accessed=12 * edges * width,
            transcendentals=edges * width,
        ),
    )(*[x if 3 <= i < 7 else pltpu.with_memory_space_constraint(x, pltpu.HBM) for i, x in enumerate(operands)])


def mesh_kernel(send_ref, own_ref, near_s_ref, far_s_ref, near_b_ref, far_b_ref, out_ref, back):
    margin = far_s_ref.shape[0]
    width = far_s_ref.shape[1]
    for pair, (near, far) in enumerate(((near_s_ref, far_s_ref), (near_b_ref, far_b_ref))):
        odd = parity("band" if pair else "sector")
        first = pl.ds(pl.multiple_of((2 * pair + 1 - odd) * margin, margin), margin)
        second = pl.ds(pl.multiple_of((2 * pair + odd) * margin, margin), margin)
        for i in range(width // near.shape[1]):
            back[first, i * near.shape[1] : (i + 1) * near.shape[1]] = near[i * margin : (i + 1) * margin, :]
        back[second, :] = far[...]
    hot = onehot_rows(send_ref[...], own_ref.shape[0])
    out_ref[...] = (own_ref[...] + mm(hot, back[...])).astype(BF16)


def mesh_grads(send_rows, own, returned):
    n, width = send_rows.shape[0], own.shape[1]

    def tail(array):
        rows = n // 4 * width // array.shape[1]
        return pl.BlockSpec((rows, array.shape[1]), lambda i: (array.shape[0] // rows - 1, 0))

    whole = lambda array: pl.BlockSpec(array.shape, lambda i: (0, 0))
    send_row = send_rows.reshape(1, n)
    return pl.pallas_call(
        mesh_kernel,
        out_shape=jax.ShapeDtypeStruct(own.shape, BF16),
        grid=(1,),
        in_specs=[whole(send_row), whole(own)] + [tail(array) for array in returned],
        out_specs=whole(own),
        scratch_shapes=[pltpu.VMEM((n, width), BF16)],
        compiler_params=pltpu.CompilerParams(vmem_limit_bytes=8 << 20),
        name="mesh_grads",
        cost_estimate=pl.CostEstimate(flops=2 * n * n * width, bytes_accessed=1 << 19, transcendentals=0),
    )(send_row, own, *returned)


def trade(part, axis, turn):
    devices = lax.axis_size(axis)
    last = devices if axis == "sector" else devices - 1
    ups = [(i, (i + 1) % devices) for i in range(turn, last, 2)]
    return lax.ppermute(part, axis, ups + [(j, i) for i, j in ups])


def swap(parts):
    return [trade(parts[2 * pair + turn], axis, turn) for pair, axis in enumerate(("sector", "band")) for turn in range(2)]


def coordinates(band, sector):
    return {
        "x_lo": band // 4,
        "y": gray(band % 4),
        "x_hi": sector // 16,
        "z": z_code(sector % 16 // 2),
        "core": sector % 2,
    }


def send(values, flips):
    place = {}
    for band in range(lax.axis_size("band")):
        for sector in range(lax.axis_size("sector")):
            place[tuple(coordinates(band, sector).values())] = band * lax.axis_size("sector") + sector
    names = list(coordinates(0, 0))
    pairs = []
    for spot, source in place.items():
        target = list(spot)
        for name, bit in flips:
            target[names.index(name)] ^= 1 << bit
        pairs.append((source, place[tuple(target)]))
    return lax.ppermute(values, ("band", "sector"), sorted(pairs))


def total(*terms):
    return sum(term.astype(F32) for term in terms).astype(BF16)


def plus(a, b):
    return total(a, b)


def reduce_weights(near_b, send_a, send_b, keep_a, keep_b, tails):
    here = coordinates(lax.axis_index("band"), lax.axis_index("sector"))

    def bit(name, k=0):
        return ((here[name] >> k) & 1) == 1

    def halve(low, high, name, k=0):
        mine = bit(name, k)
        return jnp.where(mine, high, low), send(jnp.where(mine, low, high), [(name, k)])

    def quarter(values, first, second):
        parts = values.reshape(2, 2, values.shape[0] // 4, values.shape[1])
        one, two = bit(*first), bit(*second)

        def part(swap_one, swap_two):
            low, high = (jnp.where(two != swap_two, row[1], row[0]) for row in parts)
            return jnp.where(one != swap_one, high, low)

        return part(False, False), send(part(True, False), [first]), send(part(False, True), [second]), send(part(True, True), [first, second])

    def halves(values, axis):
        return jnp.split(values, 2, axis=axis)

    near_s = got_a = send(send_a, [("core", 0)])
    part_a = plus(keep_a, got_a[: keep_a.shape[0]])
    part_b = plus(keep_b, send(send_b, [("core", 0)]))
    a, got_a = halve(*halves(part_a, 0), "z")
    left, right = halves(part_b, 1)
    mine = bit("y")
    b = jnp.where(mine, right, left)
    near_b = got_b = send(jnp.concatenate([jnp.where(mine, left, right), near_b], axis=0), [("y", 0)])
    got_b = got_b[: b.shape[0]]
    got_a, got_b = tails[0](part_b, got_a, got_b, near_s, near_b)
    a, got_a = halve(*halves(plus(a, got_a), 1), "y")
    b, got_b = halve(*halves(plus(b, got_b), 0), "z")
    got_a, got_b = tails[1](got_a, got_b)
    both = jnp.stack([plus(a, got_a).reshape(2, -1, a.shape[1]), plus(b, got_b).reshape(2, -1, a.shape[1])])
    held, *got = quarter(both.reshape(-1, a.shape[1]), ("x_lo", 0), ("z", 1))
    part = total(held, *got)
    held, *got = quarter(part, ("z", 2), ("x_hi", 0))
    part = total(held, *got)
    part = plus(part, send(part, [("y", 1)]))
    by_y = send(part, [("y", 0)])
    by_x = send(part, [("x_lo", 0)])
    by_both = send(part, [("y", 0), ("x_lo", 0)])
    odd_y, odd_x = bit("y"), bit("x_lo")

    def ordered(mine, other):
        return jnp.concatenate([jnp.where(odd_y, other, mine), jnp.where(odd_y, mine, other)], axis=1)

    near, far = ordered(part, by_y), ordered(by_x, by_both)
    return jnp.concatenate([jnp.where(odd_x, far, near), jnp.where(odd_x, near, far)], axis=1).astype(F32)


def shards(
    grid_lat,
    mesh_lat,
    edge_feat,
    edge_src,
    edge_dst,
    send_rows,
    w_edge1,
    w_edge2,
    edge_gain,
    w_node1,
    w_node2,
    node_gain,
    cotangent,
):
    lat_rows, lon_cols, width = grid_lat.shape
    grid_block = grid_lat.reshape(lat_rows * lon_cols, width)
    cot_block = cotangent.reshape(lat_rows * lon_cols, width)
    received = swap(pick(send_rows, mesh_lat))
    result, grad_grid, own_grad, far_s, near_b, far_b, *sums = main(
        edge_src, edge_dst, mesh_lat, received, edge_gain, node_gain, edge_feat, grid_block, cot_block, w_edge1, w_edge2, w_node1, w_node2
    )
    done = {}

    def after_first(part, got_a, got_b, near_s, near_b):
        far, other, _ = lax.optimization_barrier((far_s, far_b, part))
        far, other, *got = lax.optimization_barrier((trade(far, "sector", 1), trade(other, "band", 1), got_a, got_b))
        done["back"] = near_s, far, near_b, other
        return got

    def after_second(*got):
        done["mesh"], *got = lax.optimization_barrier((mesh_grads(send_rows, own_grad, done["back"]), *got))
        return got

    grad_w = reduce_weights(near_b, *sums, (after_first, after_second))
    total_edges = edge_feat.shape[0] * lax.axis_size("band") * lax.axis_size("sector")
    grad_w = grad_w * (1.0 / math.sqrt(total_edges))
    return (
        result.reshape(lat_rows, lon_cols, width),
        grad_grid.reshape(lat_rows, lon_cols, width),
        done["mesh"],
        grad_w,
    )


def solution(mesh):
    rows = P(("band", "sector"), None)
    flat = P(("band", "sector"))
    grid = P("band", "sector", None)
    in_specs = (grid, rows, rows, flat, flat, flat, P(), P(), P(), P(), P(), P(), grid)
    out_specs = (grid, grid, rows, P("sector", None))
    return jax.shard_map(shards, mesh=mesh, in_specs=in_specs, out_specs=out_specs, check_vma=False)
```
